32 devices in a mesh: ctx: 8 (over z, y), head: 4 (over x, core).
Axes of the slice: x: 2, y: 2, z: 4, core: 2. Of those that a mesh axis runs over, the one named last changes fastest.
Arguments:
- queries: bfloat16 [2048, 4096], P(('ctx', 'head')), may hold values from -6 to 6
- key_rows: bfloat16 [2048, 512], P(('ctx', 'head')), may hold values from -6 to 6
- value_rows: bfloat16 [2048, 512], P(('ctx', 'head')), may hold values from -6 to 6
- attn_out: bfloat16 [2048, 4096], P(('ctx', 'head')), may hold values from -6 to 6
- out_grad: bfloat16 [2048, 4096], P(('ctx', 'head')), may hold values from -864 to 864
- logsumexp: float32 [32, 2048], P('head', 'ctx'), may hold values from 7.5 to 8.7
Outputs:
- grad_queries: float32 [2048, 4096], P(('ctx', 'head'))
- grad_keys: float32 [2048, 512], P(('ctx', 'head'))
- grad_values: float32 [2048, 512], P(('ctx', 'head'))
The draws below stay inside these ranges and needn't reach their ends.
All inputs are finite; a program needn't handle non-finite values.
Results may differ from the reference program's by a relative error of at most 0.0051.
Values may be sent and summed in bfloat16 or wider, within the bound.
No kernel may reach another device: no remote copies, remote signals or barrier semaphores. Data moves between devices by JAX's collectives and lax.ppermute only.
A program may use at most 64 MiB of HBM per device.

```python
import math
import jax
import jax.numpy as jnp
from jax import lax

HEAD_DIM = 128
GROUP = 8
BLOCK = 256
TOKENS = 2048
KVH = 4
QH = 32
LEVELS = 3


def block_scale(own_key, extent, cuts, low, top_value):
    def one(dim, parts):
        draws = jax.random.uniform(jax.random.fold_in(jax.random.fold_in(own_key, 6), dim), (parts,), jnp.float32, low / len(cuts), top_value / len(cuts))
        return jnp.repeat(jnp.exp(draws), extent[dim] // parts).reshape((-1,) + (1,) * (len(extent) - dim - 1))

    gain = one(*cuts[0])
    for cut in cuts[1:]:
        gain = gain * one(*cut)
    return gain


def noise(key, dims, deviation, reach, cuts=(), dtype=jnp.bfloat16):
    entries = jax.random.normal(key, dims, jnp.float32) * deviation
    if len(cuts) > 0:
        entries = block_scale(key, dims, cuts, -0.22, 0.18) * entries
    return jnp.clip(entries, min=-reach, max=reach).astype(dtype)


def setup_inputs(seed: int = 0) -> dict:
    key_list = jax.random.split(jax.random.key(seed), 7)
    queries = noise(key_list[0], (TOKENS, QH * HEAD_DIM), 1.0, 6.0, ((0, 32),))
    key_rows = noise(key_list[1], (TOKENS, KVH * HEAD_DIM), 1.0, 6.0, ((0, 32),))
    value_rows = noise(key_list[2], (TOKENS, KVH * HEAD_DIM), 1.0, 6.0, ((0, 32),))
    attn_out = noise(key_list[3], (TOKENS, QH * HEAD_DIM), 1.0, 6.0, ((0, 32),))
    out_grad = noise(key_list[4], (TOKENS, QH * HEAD_DIM), (147456 // ((LEVELS + 1) * BLOCK)), 864.0, ((0, 32),))
    logsumexp = jnp.clip(7.5 + 1.1999998 * jax.random.uniform(key_list[5], (QH, TOKENS), jnp.float32) ** block_scale(key_list[5], (QH, TOKENS), ((0, 4), (1, 8)), -0.2, 0.2), 7.5, 8.7)
    return {"queries": queries, "key_rows": key_rows, "value_rows": value_rows, "attn_out": attn_out, "out_grad": out_grad, "logsumexp": logsumexp}


def flip_blocks(values_in, bit_level):
    blocks = values_in.shape[0]
    stride = 1 << bit_level
    grouped = values_in.reshape((blocks // (2 * stride), 2, stride) + values_in.shape[1:])
    return jnp.flip(grouped, axis=1).reshape(values_in.shape)

def pair_grads(pieces):
    query_blk, grad_blk, lse_rows, dot_rows, key_blk, value_blk = pieces
    score_scale = 1.0 / math.sqrt(HEAD_DIM)
    highest = lax.Precision.HIGHEST
    scores = jnp.einsum('bhgd,khd->hgbk', query_blk, key_blk, precision=highest) * score_scale
    attn_probs = jnp.exp(scores - lse_rows[..., None])
    dprobs = jnp.einsum('bhgd,khd->hgbk', grad_blk, value_blk, precision=highest)
    dscores = lax.optimization_barrier((attn_probs * (dprobs - dot_rows[..., None])).astype(jnp.bfloat16)).astype(jnp.float32)
    weights = lax.optimization_barrier(attn_probs.astype(jnp.bfloat16)).astype(jnp.float32)
    d_values = jnp.einsum('hgbk,bhgd->khd', weights, grad_blk, precision=highest)
    d_query = jnp.einsum('hgbk,khd->bhgd', dscores, key_blk, precision=highest) * score_scale
    d_keys = jnp.einsum('hgbk,bhgd->khd', dscores, query_blk, precision=highest) * score_scale
    return (d_query, d_keys, d_values)

def reference(queries, key_rows, value_rows, attn_out, out_grad, logsumexp):
    total = queries.shape[0]
    blocks = total // BLOCK
    kv_heads = key_rows.shape[1] // HEAD_DIM
    query_blk = queries.astype(jnp.float32).reshape(blocks, BLOCK, kv_heads, GROUP, HEAD_DIM)
    grad_blk = out_grad.astype(jnp.float32).reshape(blocks, BLOCK, kv_heads, GROUP, HEAD_DIM)
    out_blk = attn_out.astype(jnp.float32).reshape(blocks, BLOCK, kv_heads, GROUP, HEAD_DIM)
    dot_rows = lax.optimization_barrier(jnp.sum(grad_blk * out_blk, axis=-1)).transpose(0, 2, 3, 1)
    lse_rows = logsumexp.reshape(kv_heads, GROUP, blocks, BLOCK).transpose(2, 0, 1, 3)
    key_blk = key_rows.astype(jnp.float32).reshape(blocks, BLOCK, kv_heads, HEAD_DIM)
    value_blk = value_rows.astype(jnp.float32).reshape(blocks, BLOCK, kv_heads, HEAD_DIM)
    total_q = jnp.zeros(query_blk.shape, jnp.float32)
    total_k = jnp.zeros(key_blk.shape, jnp.float32)
    total_v = jnp.zeros(key_blk.shape, jnp.float32)
    for bit_level in range(-1, blocks.bit_length() - 1):
        if bit_level < 0:
            near_k, near_v = (key_blk, value_blk)
        else:
            near_k, near_v = (flip_blocks(key_blk, bit_level), flip_blocks(value_blk, bit_level))
        part_q, part_k, part_v = lax.map(pair_grads, (query_blk, grad_blk, lse_rows, dot_rows, near_k, near_v))
        if bit_level >= 0:
            part_k, part_v = (flip_blocks(part_k, bit_level), flip_blocks(part_v, bit_level))
        total_q = total_q + part_q
        total_k = total_k + part_k
        total_v = total_v + part_v
    return (total_q.reshape(total, -1), total_k.reshape(total, -1), total_v.reshape(total, -1))
```

```python
import functools
import math

import jax
import jax.numpy as jnp
from jax import lax
from jax.experimental import pallas as pl
from jax.experimental.pallas import tpu as pltpu
from jax.sharding import PartitionSpec as P

HEAD_DIM = 128
GROUP = 8
DOT_ROWS = 32

F32 = jnp.float32
BF16 = jnp.bfloat16


def dot_nt(a, b):
    return lax.dot_general(a, b, (((1,), (1,)), ((), ())), preferred_element_type=F32)


def dot_nn(a, b):
    return lax.dot_general(a, b, (((1,), (0,)), ((), ())), preferred_element_type=F32)


def dot_tn(a, b):
    return lax.dot_general(a, b, (((0,), (0,)), ((), ())), preferred_element_type=F32)


def vmem_specs(count):
    return [pl.BlockSpec(memory_space=pltpu.VMEM) for _ in range(count)]


def call(kernel, out_shapes, place, *args):
    return pl.pallas_call(
        kernel,
        out_shape=out_shapes,
        in_specs=[pl.BlockSpec(memory_space=pltpu.SMEM)] + vmem_specs(len(args)),
        out_specs=vmem_specs(len(out_shapes)),
    )(place, *args)


def pack_kernel(parts, place, q_ref, g_ref, o_ref, k_ref, v_ref, *outs):
    qg_refs, kv_refs = outs[:parts], outs[parts:]
    own = place[0]
    rows = q_ref.shape[0]
    width = GROUP * HEAD_DIM
    lane = lax.broadcasted_iota(jnp.int32, (2 * rows, HEAD_DIM), 1)
    dots = jnp.zeros((2 * rows, HEAD_DIM), F32)
    for m in range(parts):
        peer = own ^ m
        col = pl.multiple_of(peer * HEAD_DIM, HEAD_DIM)
        kv_refs[m][:rows, :] = k_ref[:, pl.ds(col, HEAD_DIM)]
        kv_refs[m][rows:, :] = v_ref[:, pl.ds(col, HEAD_DIM)]
        sums = []
        for j in range(GROUP):
            col = pl.multiple_of(peer * width + j * HEAD_DIM, HEAD_DIM)
            qg_refs[m][j * rows : (j + 1) * rows, :] = q_ref[:, pl.ds(col, HEAD_DIM)]
            grad = g_ref[:, pl.ds(col, HEAD_DIM)]
            qg_refs[m][(GROUP + j) * rows : (GROUP + j + 1) * rows, :] = grad
            prod = grad.astype(F32) * o_ref[:, pl.ds(col, HEAD_DIM)].astype(F32)
            sums.append(jnp.sum(prod, axis=1, keepdims=True))
        for j in range(GROUP // 2):
            pair = jnp.concatenate([sums[2 * j], sums[2 * j + 1]], axis=0)
            dots = jnp.where(lane == 8 * m + j, pair, dots)
    turned = dots.T
    for m in range(parts):
        full = turned[8 * m : 8 * m + 8, :]
        high = full.astype(BF16).astype(F32)
        mid = (full - high).astype(BF16).astype(F32)
        low = (full - high) - mid
        qg_refs[m][2 * GROUP * rows :, :] = jnp.concatenate(
            [high, mid, low, jnp.zeros_like(high)], axis=0
        ).astype(BF16)


def join_kernel(parts, place, *refs):
    pieces, out = refs[:parts], refs[parts]
    rows = pieces[0].shape[0] // 2
    for m in range(parts):
        out[m * rows : (m + 1) * rows, :] = pieces[m][:rows, :]
        out[(parts + m) * rows : (parts + m + 1) * rows, :] = pieces[m][rows:, :]


def row_of(stack):
    return jnp.concatenate([stack[j : j + 1, :] for j in range(GROUP // 2)], axis=1)


def chunk_kernel(pieces, levels, has_acc, last, place, *refs):
    count = len(pieces)
    qg_refs, refs = refs[:count], refs[count:]
    lse_ref, refs = refs[0], refs[1:]
    kv_refs, refs = refs[:levels], refs[levels:]
    if has_acc:
        acc_refs, refs = refs[:levels], refs[levels:]
    dq_refs, dkv_refs = refs[:count], refs[count:]
    scale = 1.0 / math.sqrt(HEAD_DIM)
    span = (qg_refs[0].shape[0] - DOT_ROWS) // 2
    block = kv_refs[0].shape[0] // 2
    dk = [acc_refs[b][:block, :] if has_acc else None for b in range(levels)]
    dv = [acc_refs[b][block:, :] if has_acc else None for b in range(levels)]
    for i, m in enumerate(pieces):
        query = qg_refs[i][:span, :]
        grad = qg_refs[i][span : 2 * span, :]
        split = qg_refs[i][2 * span :, :].astype(F32)
        dots = row_of((split[:8] + split[8:16]) + split[16:24])
        lse = row_of(lse_ref[place[0] ^ m])
        dq = None
        for b in range(levels):
            keys = kv_refs[b][:block, :]
            values = kv_refs[b][block:, :]
            probs = jnp.exp(dot_nt(keys, query) * scale - lse)
            dprobs = dot_nt(values, grad)
            dscores = (probs * (dprobs - dots)).astype(BF16)
            part_v = dot_nn(probs.astype(BF16), grad)
            part_k = dot_nn(dscores, query)
            part_q = dot_tn(keys, dscores)
            dv[b] = part_v if dv[b] is None else dv[b] + part_v
            dk[b] = part_k if dk[b] is None else dk[b] + part_k
            dq = part_q if dq is None else dq + part_q
        dq_refs[i][...] = (dq.T * scale).astype(dq_refs[i].dtype)
    for b in range(levels):
        dkv_refs[b][:block, :] = (dk[b] * scale if last else dk[b]).astype(dkv_refs[b].dtype)
        dkv_refs[b][block:, :] = dv[b].astype(dkv_refs[b].dtype)


def total_kernel(parts, levels, place, *refs):
    terms, outs = refs[:levels], refs[levels:]
    total = terms[0][...]
    for term in terms[1:]:
        total = total + term[...].astype(F32)
    rows = total.shape[0] // (2 * parts)
    for m in range(parts):
        outs[m][:rows, :] = total[m * rows : (m + 1) * rows].astype(outs[m].dtype)
        outs[m][rows:, :] = total[(parts + m) * rows : (parts + m + 1) * rows].astype(
            outs[m].dtype
        )


def unpack_q_kernel(parts, place, *refs):
    pieces, out = refs[:parts], refs[parts]
    rows = out.shape[0]
    width = GROUP * HEAD_DIM
    for m in range(parts):
        for j in range(GROUP):
            col = pl.multiple_of((place[0] ^ m) * width + j * HEAD_DIM, HEAD_DIM)
            out[:, pl.ds(col, HEAD_DIM)] = pieces[m][j * rows : (j + 1) * rows, :].astype(F32)


def unpack_kv_kernel(parts, place, *refs):
    pieces, out_k, out_v = refs[:parts], refs[parts], refs[parts + 1]
    rows = out_k.shape[0]
    for m in range(parts):
        col = pl.multiple_of((place[0] ^ m) * HEAD_DIM, HEAD_DIM)
        out_k[:, pl.ds(col, HEAD_DIM)] = pieces[m][:rows, :].astype(F32)
        out_v[:, pl.ds(col, HEAD_DIM)] = pieces[m][rows:, :].astype(F32)


def swap(value, axis, distance):
    return lax.ppermute(value, axis, [(i, i ^ distance) for i in range(lax.axis_size(axis))])


def on_device(queries, key_rows, value_rows, attn_out, out_grad, logsumexp):
    parts = lax.axis_size("head")
    levels = lax.axis_size("ctx").bit_length()
    rows = queries.shape[0]
    block = rows * parts
    span = rows * GROUP
    place = lax.axis_index("head").astype(jnp.int32).reshape(1)
    shape = jax.ShapeDtypeStruct

    packed = call(
        functools.partial(pack_kernel, parts),
        [shape((2 * span + DOT_ROWS, HEAD_DIM), BF16)] * parts
        + [shape((2 * rows, HEAD_DIM), BF16)] * parts,
        place,
        queries,
        out_grad,
        attn_out,
        key_rows,
        value_rows,
    )
    qg, kv = list(packed[:parts]), list(packed[parts:])
    kv = [kv[0]] + [swap(kv[m], "head", m) for m in range(1, parts)]
    qg = [qg[0]] + [swap(qg[m], "head", m) for m in range(1, parts)]
    lse = (
        logsumexp.reshape(GROUP // 2, 2, parts, rows)
        .transpose(2, 0, 1, 3)
        .reshape(parts, GROUP // 2, 2 * rows)
    )
    (kv_own,) = call(
        functools.partial(join_kernel, parts), [shape((2 * block, HEAD_DIM), BF16)], place, *kv
    )
    kv_all = [kv_own] + [swap(kv_own, "ctx", 1 << b) for b in range(levels - 1)]

    groups = [(0, 1)] + [(m,) for m in range(2, parts)]
    dq = []
    acc = []
    for step, pieces in enumerate(groups):
        last = step == len(groups) - 1
        outs = [shape((span, HEAD_DIM), F32 if m == 0 else BF16) for m in pieces]
        outs += [
            shape((2 * block, HEAD_DIM), BF16 if last and b > 0 else F32) for b in range(levels)
        ]
        result = call(
            functools.partial(chunk_kernel, pieces, levels, step > 0, last),
            outs,
            place,
            *[qg[m] for m in pieces],
            lse,
            *kv_all,
            *acc,
        )
        for i, m in enumerate(pieces):
            dq.append(result[i] if m == 0 else swap(result[i], "head", m))
        acc = list(result[len(pieces) :])

    terms = [acc[0]] + [swap(acc[b + 1], "ctx", 1 << b) for b in range(levels - 1)]
    dkv = call(
        functools.partial(total_kernel, parts, levels),
        [shape((2 * rows, HEAD_DIM), F32 if m == 0 else BF16) for m in range(parts)],
        place,
        *terms,
    )
    dkv = [dkv[0]] + [swap(dkv[m], "head", m) for m in range(1, parts)]
    (grad_q,) = call(
        functools.partial(unpack_q_kernel, parts), [shape(queries.shape, F32)], place, *dq
    )
    grad_k, grad_v = call(
        functools.partial(unpack_kv_kernel, parts),
        [shape(key_rows.shape, F32), shape(value_rows.shape, F32)],
        place,
        *dkv,
    )
    return (grad_q, grad_k, grad_v)


def solution(mesh):
    rows = P(("ctx", "head"), None)
    return jax.shard_map(
        on_device,
        mesh=mesh,
        in_specs=(rows, rows, rows, rows, rows, P("head", "ctx")),
        out_specs=(rows, rows, rows),
        check_vma=False,
    )
```

```python
import functools
import math

import jax
import jax.numpy as jnp
from jax import lax
from jax.experimental import pallas as pl
from jax.experimental.pallas import tpu as pltpu
from jax.sharding import PartitionSpec as P

HEAD_DIM = 128
GROUP = 8
PAIRS = GROUP // 2
DOT_ROWS = 32
VMEM_BYTES = 16 * 1024 * 1024

F32 = jnp.float32
BF16 = jnp.bfloat16

HEAD_ORDER = [j + half * PAIRS for j in range(PAIRS) for half in range(2)]


def dot_nt(a, b):
    return lax.dot_general(a, b, (((1,), (1,)), ((), ())), preferred_element_type=F32)


def dot_nn(a, b):
    return lax.dot_general(a, b, (((1,), (0,)), ((), ())), preferred_element_type=F32)


def dot_tn(a, b):
    return lax.dot_general(a, b, (((0,), (0,)), ((), ())), preferred_element_type=F32)


def vmem(shape, dtype):
    return pltpu.VMEM(shape, dtype)


def hbm(shape, dtype):
    return jax.ShapeDtypeStruct(shape, dtype)


def call(kernel, out_shapes, place, *args, inside=True):
    if inside:
        args = [pltpu.with_memory_space_constraint(a, pltpu.VMEM) for a in args]
    return pl.pallas_call(
        kernel,
        out_shape=out_shapes,
        in_specs=[pl.BlockSpec(memory_space=pltpu.SMEM)]
        + [pl.BlockSpec(memory_space=pltpu.VMEM) for _ in args],
        out_specs=[pl.BlockSpec(memory_space=pltpu.VMEM) for _ in out_shapes],
        compiler_params=pltpu.CompilerParams(vmem_limit_bytes=VMEM_BYTES),
    )(place, *args)


def pack_kernel(parts, place, q_ref, g_ref, o_ref, k_ref, v_ref, l_ref, *outs):
    qg_refs, kv_refs, lse_ref = outs[:parts], outs[parts : 2 * parts - 1], outs[2 * parts - 1]
    own = place[0]
    rows = q_ref.shape[0]
    width = GROUP * HEAD_DIM
    lane = lax.broadcasted_iota(jnp.int32, (2 * rows, HEAD_DIM), 1)
    dots = jnp.zeros((2 * rows, HEAD_DIM), F32)
    start = 2 * GROUP * rows + DOT_ROWS
    for m in range(parts):
        peer = own ^ m
        col = pl.multiple_of(peer * HEAD_DIM, HEAD_DIM)
        if m == 1:
            target = qg_refs[1].at[start : start + 2 * rows]
        else:
            target = kv_refs[max(m - 1, 0)]
        target[:rows, :] = k_ref[:, pl.ds(col, HEAD_DIM)]
        target[rows:, :] = v_ref[:, pl.ds(col, HEAD_DIM)]
        sums = []
        for i, h in enumerate(HEAD_ORDER):
            col = pl.multiple_of(peer * width + h * HEAD_DIM, HEAD_DIM)
            qg_refs[m][i * rows : (i + 1) * rows, :] = q_ref[:, pl.ds(col, HEAD_DIM)]
            grad = g_ref[:, pl.ds(col, HEAD_DIM)]
            qg_refs[m][(GROUP + i) * rows : (GROUP + i + 1) * rows, :] = grad
            prod = grad.astype(F32) * o_ref[:, pl.ds(col, HEAD_DIM)].astype(F32)
            sums.append(jnp.sum(prod, axis=1, keepdims=True))
        for j in range(PAIRS):
            pair = jnp.concatenate([sums[2 * j], sums[2 * j + 1]], axis=0)
            dots = jnp.where(lane == 8 * m + j, pair, dots)
    turned = dots.T
    for m in range(parts):
        full = turned[8 * m : 8 * m + 8, :]
        high = full.astype(BF16).astype(F32)
        mid = (full - high).astype(BF16).astype(F32)
        low = (full - high) - mid
        first = 2 * GROUP * rows
        qg_refs[m][first : first + DOT_ROWS, :] = jnp.concatenate(
            [high, mid, low, jnp.zeros_like(high)], axis=0
        ).astype(BF16)
    for m in range(parts):
        piece = l_ref[:, :rows]
        for c in range(1, parts):
            piece = jnp.where((own ^ m) == c, l_ref[:, c * rows : (c + 1) * rows], piece)
        piece = piece * math.log2(math.e)
        lse_ref[8 * m : 8 * m + PAIRS, :] = jnp.concatenate([piece[:PAIRS], piece[PAIRS:]], axis=1)
        lse_ref[8 * m + PAIRS : 8 * m + 8, :] = jnp.zeros((8 - PAIRS, 2 * rows), F32)


def join_kernel(parts, place, *refs):
    pieces, out = refs[:parts], refs[parts]
    rows = out.shape[0] // (2 * parts)
    for m in range(parts):
        start = pieces[m].shape[0] - 2 * rows
        out[m * rows : (m + 1) * rows, :] = pieces[m][start : start + rows, :]
        out[(parts + m) * rows : (parts + m + 1) * rows, :] = pieces[m][start + rows :, :]


def row_of(stack):
    return jnp.concatenate([stack[j : j + 1, :] for j in range(PAIRS)], axis=1)


def step_kernel(pieces, blocks, span, has_dq, has_acc, dq_done, acc_done, place, *refs):
    refs = list(refs)

    def take(count):
        out = refs[:count]
        del refs[:count]
        return out

    qg_refs = take(len(pieces))
    (lse_ref,) = take(1)
    kv_refs = take(blocks)
    dq_in = take(len(pieces)) if has_dq else None
    acc_in = take(blocks) if has_acc else None
    dq_out = take(len(pieces))
    acc_out = take(blocks)
    scale = 1.0 / math.sqrt(HEAD_DIM)
    block = kv_refs[0].shape[0] // 2
    dk = [acc_in[b][:block, :] if has_acc else None for b in range(blocks)]
    dv = [acc_in[b][block:, :] if has_acc else None for b in range(blocks)]
    for i, m in enumerate(pieces):
        query = qg_refs[i][:span, :]
        grad = qg_refs[i][span : 2 * span, :]
        split = qg_refs[i][2 * span : 2 * span + DOT_ROWS, :].astype(F32)
        dots = row_of((split[:8] + split[8:16]) + split[16:24])
        lse = row_of(lse_ref[8 * m : 8 * m + 8, :])
        dq = dq_in[i][...] if has_dq else None
        for b in range(blocks):
            keys = kv_refs[b][:block, :]
            values = kv_refs[b][block:, :]
            probs = jnp.exp2(dot_nt(keys, query) * (scale * math.log2(math.e)) - lse)
            dprobs = dot_nt(values, grad)
            dscores = (probs * (dprobs - dots)).astype(BF16)
            part_v = dot_nn(probs.astype(BF16), grad)
            part_k = dot_nn(dscores, query)
            part_q = dot_tn(keys, dscores)
            dv[b] = part_v if dv[b] is None else dv[b] + part_v
            dk[b] = part_k if dk[b] is None else dk[b] + part_k
            dq = part_q if dq is None else dq + part_q
        if dq_done:
            dq_out[i][...] = (dq.T * scale).astype(dq_out[i].dtype)
        else:
            dq_out[i][...] = dq
    for b in range(blocks):
        acc_out[b][:block, :] = (dk[b] * scale if acc_done else dk[b]).astype(acc_out[b].dtype)
        acc_out[b][block:, :] = dv[b].astype(acc_out[b].dtype)


def total_kernel(parts, levels, place, *refs):
    terms, outs = refs[:levels], refs[levels:]
    total = terms[0][...]
    for term in terms[1:]:
        total = total + term[...].astype(F32)
    rows = total.shape[0] // (2 * parts)
    for m in range(parts):
        outs[m][:rows, :] = total[m * rows : (m + 1) * rows].astype(outs[m].dtype)
        outs[m][rows:, :] = total[(parts + m) * rows : (parts + m + 1) * rows].astype(
            outs[m].dtype
        )


def unpack_q_kernel(parts, place, *refs):
    pieces, out = refs[:parts], refs[parts]
    rows = out.shape[0]
    width = GROUP * HEAD_DIM
    for m in range(parts):
        for i, h in enumerate(HEAD_ORDER):
            col = pl.multiple_of((place[0] ^ m) * width + h * HEAD_DIM, HEAD_DIM)
            out[:, pl.ds(col, HEAD_DIM)] = pieces[m][i * rows : (i + 1) * rows, :].astype(F32)


def unpack_kv_kernel(parts, place, *refs):
    pieces, out_k, out_v = refs[:parts], refs[parts], refs[parts + 1]
    rows = out_k.shape[0]
    for m in range(parts):
        col = pl.multiple_of((place[0] ^ m) * HEAD_DIM, HEAD_DIM)
        out_k[:, pl.ds(col, HEAD_DIM)] = pieces[m][:rows, :].astype(F32)
        out_v[:, pl.ds(col, HEAD_DIM)] = pieces[m][rows:, :].astype(F32)


def swap(value, axis, distance):
    return lax.ppermute(value, axis, [(i, i ^ distance) for i in range(lax.axis_size(axis))])


def on_device(queries, key_rows, value_rows, attn_out, out_grad, logsumexp):
    parts = lax.axis_size("head")
    levels = lax.axis_size("ctx").bit_length()
    rows = queries.shape[0]
    block = rows * parts
    span = rows * GROUP
    place = lax.axis_index("head").astype(jnp.int32).reshape(1)

    sizes = [2 * span + DOT_ROWS + (2 * rows if m == 1 else 0) for m in range(parts)]
    packed = call(
        functools.partial(pack_kernel, parts),
        [vmem((size, HEAD_DIM), BF16) for size in sizes]
        + [vmem((2 * rows, HEAD_DIM), BF16)] * (parts - 1)
        + [vmem((8 * parts, 2 * rows), F32)],
        place,
        queries,
        out_grad,
        attn_out,
        key_rows,
        value_rows,
        logsumexp,
        inside=False,
    )
    qg, kv, lse = list(packed[:parts]), list(packed[parts:-1]), packed[-1]
    kv = [kv[0], None] + [swap(kv[m - 1], "head", m) for m in range(2, parts)]
    qg = [qg[0]] + [swap(qg[m], "head", m) for m in range(1, parts)]
    kv[1] = qg[1]
    (kv_own,) = call(
        functools.partial(join_kernel, parts), [vmem((2 * block, HEAD_DIM), BF16)], place, *kv
    )
    kv_all = [kv_own] + [swap(kv_own, "ctx", 1 << b) for b in range(levels - 1)]

    dq = [None] * parts
    acc = [None] * levels

    def step(pieces, blocks, dq_done, acc_done):
        has_dq = dq[pieces[0]] is not None
        has_acc = acc[blocks[0]] is not None
        outs = []
        for m in pieces:
            if dq_done:
                outs.append(vmem((span, HEAD_DIM), F32 if m == 0 else BF16))
            else:
                outs.append(vmem((HEAD_DIM, span), F32))
        for b in blocks:
            outs.append(vmem((2 * block, HEAD_DIM), BF16 if acc_done and b > 0 else F32))
        result = call(
            functools.partial(
                step_kernel, pieces, len(blocks), span, has_dq, has_acc, dq_done, acc_done
            ),
            outs,
            place,
            *[qg[m] for m in pieces],
            lse,
            *[kv_all[b] for b in blocks],
            *([dq[m] for m in pieces] if has_dq else []),
            *([acc[b] for b in blocks] if has_acc else []),
        )
        for i, m in enumerate(pieces):
            dq[m] = result[i]
            if dq_done and m > 0:
                dq[m] = swap(dq[m], "head", m)
        for i, b in enumerate(blocks):
            acc[b] = result[len(pieces) + i]
            if acc_done and b > 0:
                acc[b] = swap(acc[b], "ctx", 1 << (b - 1))

    for b in range(levels):
        step((0, 1), (b,), b == levels - 1, False)
    for m in range(2, parts - 1):
        step((m,), tuple(range(levels)), True, False)
    for b in reversed(range(levels)):
        step((parts - 1,), (b,), b == 0, True)

    dkv = call(
        functools.partial(total_kernel, parts, levels),
        [vmem((2 * rows, HEAD_DIM), F32 if m == 0 else BF16) for m in range(parts)],
        place,
        *acc,
    )
    dkv = [dkv[0]] + [swap(dkv[m], "head", m) for m in range(1, parts)]
    (grad_q,) = call(
        functools.partial(unpack_q_kernel, parts), [hbm(queries.shape, F32)], place, *dq
    )
    grad_k, grad_v = call(
        functools.partial(unpack_kv_kernel, parts),
        [hbm(key_rows.shape, F32), hbm(value_rows.shape, F32)],
        place,
        *dkv,
    )
    return (grad_q, grad_k, grad_v)


def solution(mesh):
    rows = P(("ctx", "head"), None)
    return jax.shard_map(
        on_device,
        mesh=mesh,
        in_specs=(rows, rows, rows, rows, rows, P("head", "ctx")),
        out_specs=(rows, rows, rows),
        check_vma=False,
    )
```

```python
import functools
import math

import jax
import jax.numpy as jnp
from jax import lax
from jax.experimental import pallas as pl
from jax.experimental.pallas import tpu as pltpu
from jax.sharding import PartitionSpec as P


HEAD_DIM = 128
GROUP = 8
PAIRS = GROUP // 2
DOT_ROWS = 32
VMEM_BYTES = 16 * 1024 * 1024


F32 = jnp.float32
BF16 = jnp.bfloat16

HEAD_ORDER = [j + half * PAIRS for j in range(PAIRS) for half in range(2)]


def dot_nt(a, b):
    return lax.dot_general(a, b, (((1,), (1,)), ((), ())), preferred_element_type=F32)


def dot_nn(a, b):
    return lax.dot_general(a, b, (((1,), (0,)), ((), ())), preferred_element_type=F32)


def dot_tn(a, b):
    return lax.dot_general(a, b, (((0,), (0,)), ((), ())), preferred_element_type=F32)


def vmem(shape, dtype):
    return pltpu.VMEM(shape, dtype)


def hbm(shape, dtype):
    return jax.ShapeDtypeStruct(shape, dtype)


def call(kernel, out_shapes, place, *args, space=pltpu.VMEM, scratch=()):
    args = [pltpu.with_memory_space_constraint(a, space) for a in args]
    return pl.pallas_call(
        kernel,
        out_shape=out_shapes,
        in_specs=[pl.BlockSpec(memory_space=pltpu.SMEM)]
        + [pl.BlockSpec(memory_space=space) for _ in args],
        out_specs=[pl.BlockSpec(memory_space=pltpu.VMEM) for _ in out_shapes],
        scratch_shapes=scratch,
        compiler_params=pltpu.CompilerParams(vmem_limit_bytes=VMEM_BYTES),
    )(place, *args)


def load_kernel(parts, place, q_any, g_any, o_any, k_any, v_any, l_any, *refs):
    q_ref, g_ref, o_ref = refs[:3]
    kv_refs, lse_ref = refs[3 : 3 + parts], refs[3 + parts]
    k_ref, v_ref, l_ref, sems = refs[4 + parts :]
    own = place[0]
    rows = k_ref.shape[0]
    copies = [
        pltpu.make_async_copy(source, target, sems.at[i])
        for i, (source, target) in enumerate(
            [
                (k_any, k_ref),
                (v_any, v_ref),
                (l_any, l_ref),
                (q_any, q_ref),
                (g_any, g_ref),
                (o_any, o_ref),
            ]
        )
    ]
    for copy in copies:
        copy.start()
    copies[0].wait()
    copies[1].wait()
    for m in range(parts):
        col = pl.multiple_of((own ^ m) * HEAD_DIM, HEAD_DIM)
        kv_refs[m][:rows, :] = k_ref[:, pl.ds(col, HEAD_DIM)]
        kv_refs[m][rows:, :] = v_ref[:, pl.ds(col, HEAD_DIM)]
    copies[2].wait()
    for m in range(parts):
        piece = l_ref[:, :rows]
        for c in range(1, parts):
            piece = jnp.where((own ^ m) == c, l_ref[:, c * rows : (c + 1) * rows], piece)
        piece = piece * math.log2(math.e)
        lse_ref[8 * m : 8 * m + PAIRS, :] = jnp.concatenate([piece[:PAIRS], piece[PAIRS:]], axis=1)
        lse_ref[8 * m + PAIRS : 8 * m + 8, :] = jnp.zeros((8 - PAIRS, 2 * rows), F32)
    for copy in copies[3:]:
        copy.wait()


def pack_kernel(parts, place, q_ref, g_ref, o_ref, kv_ref, *qg_refs):
    own = place[0]
    rows = q_ref.shape[0]
    width = GROUP * HEAD_DIM
    lane = lax.broadcasted_iota(jnp.int32, (2 * rows, HEAD_DIM), 1)
    dots = jnp.zeros((2 * rows, HEAD_DIM), F32)
    qg_refs[1][2 * GROUP * rows + DOT_ROWS :, :] = kv_ref[...]
    for m in range(parts):
        peer = own ^ m
        sums = []
        for i, h in enumerate(HEAD_ORDER):
            col = pl.multiple_of(peer * width + h * HEAD_DIM, HEAD_DIM)
            qg_refs[m][i * rows : (i + 1) * rows, :] = q_ref[:, pl.ds(col, HEAD_DIM)]
            grad = g_ref[:, pl.ds(col, HEAD_DIM)]
            qg_refs[m][(GROUP + i) * rows : (GROUP + i + 1) * rows, :] = grad
            prod = grad.astype(F32) * o_ref[:, pl.ds(col, HEAD_DIM)].astype(F32)
            sums.append(jnp.sum(prod, axis=1, keepdims=True))
        for j in range(PAIRS):
            pair = jnp.concatenate([sums[2 * j], sums[2 * j + 1]], axis=0)
            dots = jnp.where(lane == 8 * m + j, pair, dots)
    turned = dots.T
    for m in range(parts):
        full = turned[8 * m : 8 * m + 8, :]
        high = full.astype(BF16).astype(F32)
        mid = (full - high).astype(BF16).astype(F32)
        low = (full - high) - mid
        first = 2 * GROUP * rows
        qg_refs[m][first : first + DOT_ROWS, :] = jnp.concatenate(
            [high, mid, low, jnp.zeros_like(high)], axis=0
        ).astype(BF16)


def join_kernel(parts, place, *refs):
    pieces, out = refs[:parts], refs[parts]
    rows = out.shape[0] // (2 * parts)
    for m in range(parts):
        start = pieces[m].shape[0] - 2 * rows
        out[m * rows : (m + 1) * rows, :] = pieces[m][start : start + rows, :]
        out[(parts + m) * rows : (parts + m + 1) * rows, :] = pieces[m][start + rows :, :]


def row_of(stack):
    return jnp.concatenate([stack[j : j + 1, :] for j in range(PAIRS)], axis=1)


def step_kernel(pieces, blocks, span, has_dq, has_acc, dq_done, acc_done, place, *refs):
    refs = list(refs)

    def take(count):
        out = refs[:count]
        del refs[:count]
        return out

    qg_refs = take(len(pieces))
    (lse_ref,) = take(1)
    kv_refs = take(blocks)
    dq_in = take(len(pieces)) if has_dq else None
    acc_in = take(blocks) if has_acc else None
    dq_out = take(len(pieces))
    acc_out = take(blocks)
    scale = 1.0 / math.sqrt(HEAD_DIM)
    block = kv_refs[0].shape[0] // 2
    dk = [acc_in[b][:block, :] if has_acc else None for b in range(blocks)]
    dv = [acc_in[b][block:, :] if has_acc else None for b in range(blocks)]
    for i, m in enumerate(pieces):
        query = qg_refs[i][:span, :]
        grad = qg_refs[i][span : 2 * span, :]
        split = qg_refs[i][2 * span : 2 * span + DOT_ROWS, :].astype(F32)
        dots = row_of((split[:8] + split[8:16]) + split[16:24])
        lse = row_of(lse_ref[8 * m : 8 * m + 8, :])
        dq = dq_in[i][...] if has_dq else None
        for b in range(blocks):
            keys = kv_refs[b][:block, :]
            values = kv_refs[b][block:, :]
            probs = jnp.exp2(dot_nt(keys, query) * (scale * math.log2(math.e)) - lse)
            dprobs = dot_nt(values, grad)
            dscores = (probs * (dprobs - dots)).astype(BF16)
            part_v = dot_nn(probs.astype(BF16), grad)
            part_k = dot_nn(dscores, query)
            part_q = dot_tn(keys, dscores)
            dv[b] = part_v if dv[b] is None else dv[b] + part_v
            dk[b] = part_k if dk[b] is None else dk[b] + part_k
            dq = part_q if dq is None else dq + part_q
        if dq_done:
            dq_out[i][...] = (dq.T * scale).astype(dq_out[i].dtype)
        else:
            dq_out[i][...] = dq
    for b in range(blocks):
        acc_out[b][:block, :] = (dk[b] * scale if acc_done else dk[b]).astype(acc_out[b].dtype)
        acc_out[b][block:, :] = dv[b].astype(acc_out[b].dtype)


def total_kernel(parts, levels, place, *refs):
    terms, outs = refs[:levels], refs[levels:]
    total = terms[0][...]
    for term in terms[1:]:
        total = total + term[...].astype(F32)
    rows = total.shape[0] // (2 * parts)
    for m in range(parts):
        outs[m][:rows, :] = total[m * rows : (m + 1) * rows].astype(outs[m].dtype)
        outs[m][rows:, :] = total[(parts + m) * rows : (parts + m + 1) * rows].astype(
            outs[m].dtype
        )


def unpack_q_kernel(parts, place, *refs):
    pieces, out = refs[:parts], refs[parts]
    rows = out.shape[0]
    width = GROUP * HEAD_DIM
    for m in range(parts):
        for i, h in enumerate(HEAD_ORDER):
            col = pl.multiple_of((place[0] ^ m) * width + h * HEAD_DIM, HEAD_DIM)
            out[:, pl.ds(col, HEAD_DIM)] = pieces[m][i * rows : (i + 1) * rows, :].astype(F32)


def unpack_kv_kernel(parts, place, *refs):
    pieces, out_k, out_v = refs[:parts], refs[parts], refs[parts + 1]
    rows = out_k.shape[0]
    for m in range(parts):
        col = pl.multiple_of((place[0] ^ m) * HEAD_DIM, HEAD_DIM)
        out_k[:, pl.ds(col, HEAD_DIM)] = pieces[m][:rows, :].astype(F32)
        out_v[:, pl.ds(col, HEAD_DIM)] = pieces[m][rows:, :].astype(F32)


def swap(value, axis, distance):
    return lax.ppermute(value, axis, [(i, i ^ distance) for i in range(lax.axis_size(axis))])


def on_device(queries, key_rows, value_rows, attn_out, out_grad, logsumexp):
    parts = lax.axis_size("head")
    levels = lax.axis_size("ctx").bit_length()
    rows = queries.shape[0]
    block = rows * parts
    span = rows * GROUP
    place = lax.axis_index("head").astype(jnp.int32).reshape(1)

    loaded = call(
        functools.partial(load_kernel, parts),
        [vmem(queries.shape, BF16)] * 3
        + [vmem((2 * rows, HEAD_DIM), BF16)] * parts
        + [vmem((8 * parts, 2 * rows), F32)],
        place,
        queries,
        out_grad,
        attn_out,
        key_rows,
        value_rows,
        logsumexp,
        space=pltpu.HBM,
        scratch=[
            vmem(key_rows.shape, BF16),
            vmem(value_rows.shape, BF16),
            vmem(logsumexp.shape, F32),
            pltpu.SemaphoreType.DMA((6,)),
        ],
    )
    kv, lse = list(loaded[3:-1]), loaded[-1]
    sizes = [2 * span + DOT_ROWS + (2 * rows if m == 1 else 0) for m in range(parts)]
    qg = call(
        functools.partial(pack_kernel, parts),
        [vmem((size, HEAD_DIM), BF16) for size in sizes],
        place,
        *loaded[:3],
        kv[1],
    )
    qg = [qg[0]] + [swap(qg[m], "head", m) for m in range(1, parts)]
    kv = [kv[0], qg[1]] + [swap(kv[m], "head", m) for m in range(2, parts)]
    (kv_own,) = call(
        functools.partial(join_kernel, parts), [vmem((2 * block, HEAD_DIM), BF16)], place, *kv
    )
    kv_all = [kv_own] + [swap(kv_own, "ctx", 1 << (b - 1)) for b in range(1, levels)]

    dq = [None] * parts
    acc = [None] * levels

    def step(pieces, blocks, dq_done, acc_done):
        has_dq = dq[pieces[0]] is not None
        has_acc = acc[blocks[0]] is not None
        outs = []
        for m in pieces:
            if dq_done:
                outs.append(vmem((span, HEAD_DIM), F32 if m == 0 else BF16))
            else:
                outs.append(vmem((HEAD_DIM, span), F32))
        for b in blocks:
            outs.append(vmem((2 * block, HEAD_DIM), BF16 if acc_done and b > 0 else F32))
        result = call(
            functools.partial(
                step_kernel, pieces, len(blocks), span, has_dq, has_acc, dq_done, acc_done
            ),
            outs,
            place,
            *[qg[m] for m in pieces],
            lse,
            *[kv_all[b] for b in blocks],
            *([dq[m] for m in pieces] if has_dq else []),
            *([acc[b] for b in blocks] if has_acc else []),
        )
        for i, m in enumerate(pieces):
            dq[m] = result[i]
            if dq_done and m > 0:
                dq[m] = swap(dq[m], "head", m)
        for i, b in enumerate(blocks):
            acc[b] = result[len(pieces) + i]
            if acc_done and b > 0:
                acc[b] = swap(acc[b], "ctx", 1 << (b - 1))

    for b in range(levels):
        step((0, 1), (b,), b == levels - 1, False)
    for m in range(2, parts - 1):
        step((m,), tuple(range(levels)), True, False)
    for b in reversed(range(levels)):
        step((parts - 1,), (b,), b == 0, True)

    dkv = call(
        functools.partial(total_kernel, parts, levels),
        [vmem((2 * rows, HEAD_DIM), F32 if m == 0 else BF16) for m in range(parts)],
        place,
        *acc,
    )
    dkv = [dkv[0]] + [swap(dkv[m], "head", m) for m in range(1, parts)]
    (grad_q,) = call(
        functools.partial(unpack_q_kernel, parts), [hbm(queries.shape, F32)], place, *dq
    )
    grad_k, grad_v = call(
        functools.partial(unpack_kv_kernel, parts),
        [hbm(key_rows.shape, F32), hbm(value_rows.shape, F32)],
        place,
        *dkv,
    )
    return (grad_q, grad_k, grad_v)


def solution(mesh):
    rows = P(("ctx", "head"), None)
    return jax.shard_map(
        on_device,
        mesh=mesh,
        in_specs=(rows, rows, rows, rows, rows, P("head", "ctx")),
        out_specs=(rows, rows, rows),
        check_vma=False,
    )
```

```python
import functools
import math

import jax
import jax.numpy as jnp
from jax import lax
from jax.experimental import pallas as pl
from jax.experimental.pallas import tpu as pltpu
from jax.sharding import PartitionSpec as P


HEAD_DIM = 128
GROUP = 8
PAIRS = GROUP // 2
DOT_ROWS = 32
VMEM_BYTES = 16 * 1024 * 1024


F32 = jnp.float32
BF16 = jnp.bfloat16

HEAD_ORDER = [j + half * PAIRS for j in range(PAIRS) for half in range(2)]


def dot_nt(a, b):
    return lax.dot_general(a, b, (((1,), (1,)), ((), ())), preferred_element_type=F32)


def dot_nn(a, b):
    return lax.dot_general(a, b, (((1,), (0,)), ((), ())), preferred_element_type=F32)


def dot_tn(a, b):
    return lax.dot_general(a, b, (((0,), (0,)), ((), ())), preferred_element_type=F32)


def vmem(shape, dtype):
    return pltpu.VMEM(shape, dtype)


def hbm(shape, dtype):
    return jax.ShapeDtypeStruct(shape, dtype)


def call(kernel, out_shapes, place, *args, space=pltpu.VMEM, scratch=()):
    args = [pltpu.with_memory_space_constraint(a, space) for a in args]
    return pl.pallas_call(
        kernel,
        out_shape=out_shapes,
        in_specs=[pl.BlockSpec(memory_space=pltpu.SMEM)]
        + [pl.BlockSpec(memory_space=space) for _ in args],
        out_specs=[pl.BlockSpec(memory_space=pltpu.VMEM) for _ in out_shapes],
        scratch_shapes=scratch,
        compiler_params=pltpu.CompilerParams(vmem_limit_bytes=VMEM_BYTES),
    )(place, *args)


def load_kernel(parts, place, q_any, g_any, o_any, k_any, v_any, l_any, *refs):
    q_ref, g_ref, o_ref = refs[:3]
    kv_refs, lse_ref = refs[3 : 3 + parts], refs[3 + parts]
    k_ref, v_ref, l_ref, sems = refs[4 + parts :]
    own = place[0]
    rows = k_ref.shape[0]
    pairs = [(k_any, k_ref), (v_any, v_ref), (l_any, l_ref)]
    pairs += [(q_any, q_ref), (g_any, g_ref), (o_any, o_ref)]
    copies = [
        pltpu.make_async_copy(source, target, sems.at[i])
        for i, (source, target) in enumerate(pairs)
    ]
    for copy in copies:
        copy.start()
    for copy in copies[:3]:
        copy.wait()
    for m in range(parts):
        col = pl.multiple_of((own ^ m) * HEAD_DIM, HEAD_DIM)
        kv_refs[m][:rows, :] = k_ref[:, pl.ds(col, HEAD_DIM)]
        kv_refs[m][rows:, :] = v_ref[:, pl.ds(col, HEAD_DIM)]
    for m in range(parts):
        piece = l_ref[:, :rows]
        for c in range(1, parts):
            piece = jnp.where((own ^ m) == c, l_ref[:, c * rows : (c + 1) * rows], piece)
        piece = piece * math.log2(math.e)
        lse_ref[8 * m : 8 * m + PAIRS, :] = jnp.concatenate([piece[:PAIRS], piece[PAIRS:]], axis=1)
        lse_ref[8 * m + PAIRS : 8 * m + 8, :] = jnp.zeros((8 - PAIRS, 2 * rows), F32)
    for copy in copies[3:]:
        copy.wait()


def pack_kernel(m, place, q_ref, g_ref, o_ref, qg_ref):
    rows = q_ref.shape[0]
    span = GROUP * rows
    base = (place[0] ^ m) * (GROUP * HEAD_DIM)
    lane = lax.broadcasted_iota(jnp.int32, (2 * rows, HEAD_DIM), 1)
    dots = jnp.zeros((2 * rows, HEAD_DIM), F32)
    sums = []
    for i, h in enumerate(HEAD_ORDER):
        col = pl.multiple_of(base + h * HEAD_DIM, HEAD_DIM)
        qg_ref[i * rows : (i + 1) * rows, :] = q_ref[:, pl.ds(col, HEAD_DIM)]
        grad = g_ref[:, pl.ds(col, HEAD_DIM)]
        qg_ref[span + i * rows : span + (i + 1) * rows, :] = grad
        prod = grad.astype(F32) * o_ref[:, pl.ds(col, HEAD_DIM)].astype(F32)
        sums.append(jnp.sum(prod, axis=1, keepdims=True))
    for j in range(PAIRS):
        pair = jnp.concatenate([sums[2 * j], sums[2 * j + 1]], axis=0)
        dots = jnp.where(lane == j, pair, dots)
    full = dots.T[:8, :]
    high = full.astype(BF16).astype(F32)
    mid = (full - high).astype(BF16).astype(F32)
    low = (full - high) - mid
    qg_ref[2 * span :, :] = jnp.concatenate([high, mid, low, jnp.zeros_like(high)], axis=0).astype(
        BF16
    )


def join_kernel(parts, place, *refs):
    pieces, out = refs[:parts], refs[parts]
    rows = out.shape[0] // (2 * parts)
    for m in range(parts):
        out[m * rows : (m + 1) * rows, :] = pieces[m][:rows, :]
        out[(parts + m) * rows : (parts + m + 1) * rows, :] = pieces[m][rows:, :]


def row_of(stack):
    return jnp.concatenate([stack[j : j + 1, :] for j in range(PAIRS)], axis=1)


def step_kernel(pieces, blocks, span, has_dq, has_acc, dq_done, acc_done, place, *refs):
    refs = list(refs)

    def take(count):
        out = refs[:count]
        del refs[:count]
        return out

    qg_refs = take(len(pieces))
    (lse_ref,) = take(1)
    kv_refs = take(blocks)
    dq_in = take(len(pieces)) if has_dq else None
    acc_in = take(blocks) if has_acc else None
    dq_out = take(len(pieces))
    acc_out = take(blocks)
    scale = 1.0 / math.sqrt(HEAD_DIM)
    block = kv_refs[0].shape[0] // 2
    dk = [acc_in[b][:block, :] if has_acc else None for b in range(blocks)]
    dv = [acc_in[b][block:, :] if has_acc else None for b in range(blocks)]
    for i, m in enumerate(pieces):
        query = qg_refs[i][:span, :]
        grad = qg_refs[i][span : 2 * span, :]
        split = qg_refs[i][2 * span : 2 * span + DOT_ROWS, :].astype(F32)
        dots = row_of((split[:8] + split[8:16]) + split[16:24])
        lse = row_of(lse_ref[8 * m : 8 * m + 8, :])
        dq = dq_in[i][...] if has_dq else None
        for b in range(blocks):
            keys = kv_refs[b][:block, :]
            values = kv_refs[b][block:, :]
            probs = jnp.exp2(dot_nt(keys, query) * (scale * math.log2(math.e)) - lse)
            dprobs = dot_nt(values, grad)
            dscores = (probs * (dprobs - dots)).astype(BF16)
            part_v = dot_nn(probs.astype(BF16), grad)
            part_k = dot_nn(dscores, query)
            part_q = dot_tn(keys, dscores)
            dv[b] = part_v if dv[b] is None else dv[b] + part_v
            dk[b] = part_k if dk[b] is None else dk[b] + part_k
            dq = part_q if dq is None else dq + part_q
        if dq_done:
            dq_out[i][...] = (dq.T * scale).astype(dq_out[i].dtype)
        else:
            dq_out[i][...] = dq
    for b in range(blocks):
        acc_out[b][:block, :] = (dk[b] * scale if acc_done else dk[b]).astype(acc_out[b].dtype)
        acc_out[b][block:, :] = dv[b].astype(acc_out[b].dtype)


def total_kernel(parts, levels, place, *refs):
    terms, near_dq, outs = refs[:levels], refs[levels], refs[levels + 1 :]
    total = terms[0][...]
    for term in terms[1:]:
        total = total + term[...].astype(F32)
    rows = total.shape[0] // (2 * parts)
    for m in range(parts):
        outs[m][:rows, :] = total[m * rows : (m + 1) * rows].astype(outs[m].dtype)
        outs[m][rows : 2 * rows, :] = total[(parts + m) * rows : (parts + m + 1) * rows].astype(
            outs[m].dtype
        )
    outs[1][2 * rows :, :] = near_dq[...]


def unpack_q_kernel(parts, place, *refs):
    pieces, out = refs[:parts], refs[parts]
    rows = out.shape[0]
    width = GROUP * HEAD_DIM
    for m in range(parts):
        for i, h in enumerate(HEAD_ORDER):
            col = pl.multiple_of((place[0] ^ m) * width + h * HEAD_DIM, HEAD_DIM)
            first = pieces[m].shape[0] - GROUP * rows + i * rows
            out[:, pl.ds(col, HEAD_DIM)] = pieces[m][first : first + rows, :].astype(F32)


def unpack_kv_kernel(parts, place, *refs):
    pieces, out_k, out_v = refs[:parts], refs[parts], refs[parts + 1]
    rows = out_k.shape[0]
    for m in range(parts):
        col = pl.multiple_of((place[0] ^ m) * HEAD_DIM, HEAD_DIM)
        out_k[:, pl.ds(col, HEAD_DIM)] = pieces[m][:rows, :].astype(F32)
        out_v[:, pl.ds(col, HEAD_DIM)] = pieces[m][rows : 2 * rows, :].astype(F32)


def swap(value, axis, distance):
    return lax.ppermute(value, axis, [(i, i ^ distance) for i in range(lax.axis_size(axis))])


def on_device(queries, key_rows, value_rows, attn_out, out_grad, logsumexp):
    parts = lax.axis_size("head")
    levels = lax.axis_size("ctx").bit_length()
    rows = queries.shape[0]
    block = rows * parts
    span = rows * GROUP
    place = lax.axis_index("head").astype(jnp.int32).reshape(1)

    *rows_in, lse = call(
        functools.partial(load_kernel, parts),
        [vmem(queries.shape, BF16)] * 3
        + [vmem((2 * rows, HEAD_DIM), BF16)] * parts
        + [vmem((8 * parts, 2 * rows), F32)],
        place,
        queries,
        out_grad,
        attn_out,
        key_rows,
        value_rows,
        logsumexp,
        space=pltpu.HBM,
        scratch=[
            vmem(key_rows.shape, BF16),
            vmem(value_rows.shape, BF16),
            vmem(logsumexp.shape, F32),
            pltpu.SemaphoreType.DMA((6,)),
        ],
    )
    kv = rows_in[3:]
    qg = []
    for m in range(parts):
        (packed,) = call(
            functools.partial(pack_kernel, m),
            [vmem((2 * span + DOT_ROWS, HEAD_DIM), BF16)],
            place,
            *rows_in[:3],
        )
        qg.append(packed if m == 0 else swap(packed, "head", m))
    kv = [kv[0]] + [swap(kv[m], "head", m) for m in range(1, parts)]
    (kv_own,) = call(
        functools.partial(join_kernel, parts), [vmem((2 * block, HEAD_DIM), BF16)], place, *kv
    )
    kv_all = [kv_own] + [swap(kv_own, "ctx", 1 << (b - 1)) for b in range(1, levels)]

    dq = [None] * parts
    acc = [None] * levels

    def step(pieces, blocks, dq_done, acc_done):
        has_dq = dq[pieces[0]] is not None
        has_acc = acc[blocks[0]] is not None
        outs = []
        for m in pieces:
            if dq_done:
                outs.append(vmem((span, HEAD_DIM), F32 if m == 0 else BF16))
            else:
                outs.append(vmem((HEAD_DIM, span), F32))
        for b in blocks:
            outs.append(vmem((2 * block, HEAD_DIM), BF16 if acc_done and b > 0 else F32))
        result = call(
            functools.partial(
                step_kernel, pieces, len(blocks), span, has_dq, has_acc, dq_done, acc_done
            ),
            outs,
            place,
            *[qg[m] for m in pieces],
            lse,
            *[kv_all[b] for b in blocks],
            *([dq[m] for m in pieces] if has_dq else []),
            *([acc[b] for b in blocks] if has_acc else []),
        )
        for i, m in enumerate(pieces):
            dq[m] = result[i]
            if dq_done and m > 1:
                dq[m] = swap(dq[m], "head", m)
        for i, b in enumerate(blocks):
            acc[b] = result[len(pieces) + i]
            if acc_done and b > 0:
                acc[b] = swap(acc[b], "ctx", 1 << (b - 1))

    early = tuple(range(parts - 1))
    step((0,), (0,), False, False)
    step(early[1:], (0,), False, False)
    for b in range(1, levels):
        step(early, (b,), b == levels - 1, False)
    for b in reversed(range(levels)):
        step((parts - 1,), (b,), b == 0, True)

    dkv = call(
        functools.partial(total_kernel, parts, levels),
        [
            vmem((2 * rows + (span if m == 1 else 0), HEAD_DIM), F32 if m == 0 else BF16)
            for m in range(parts)
        ],
        place,
        *acc,
        dq[1],
    )
    dkv = [dkv[0]] + [swap(dkv[m], "head", m) for m in range(1, parts)]
    dq[1] = dkv[1]
    (grad_q,) = call(
        functools.partial(unpack_q_kernel, parts), [hbm(queries.shape, F32)], place, *dq
    )
    grad_k, grad_v = call(
        functools.partial(unpack_kv_kernel, parts),
        [hbm(key_rows.shape, F32), hbm(value_rows.shape, F32)],
        place,
        *dkv,
    )
    return (grad_q, grad_k, grad_v)


def solution(mesh):
    rows = P(("ctx", "head"), None)
    return jax.shard_map(
        on_device,
        mesh=mesh,
        in_specs=(rows, rows, rows, rows, rows, P("head", "ctx")),
        out_specs=(rows, rows, rows),
        check_vma=False,
    )
```

```python
import functools
import math

import jax
import jax.numpy as jnp
from jax import lax
from jax.experimental import pallas as pl
from jax.experimental.pallas import tpu as pltpu
from jax.sharding import PartitionSpec as P


HEAD_DIM = 128
GROUP = 8
PAIRS = GROUP // 2
DOT_ROWS = 32
VMEM_BYTES = 16 * 1024 * 1024


F32 = jnp.float32
BF16 = jnp.bfloat16

HEAD_ORDER = [j + half * PAIRS for j in range(PAIRS) for half in range(2)]


def dot_nt(a, b):
    return lax.dot_general(a, b, (((1,), (1,)), ((), ())), preferred_element_type=F32)


def dot_nn(a, b):
    return lax.dot_general(a, b, (((1,), (0,)), ((), ())), preferred_element_type=F32)


def dot_tn(a, b):
    return lax.dot_general(a, b, (((0,), (0,)), ((), ())), preferred_element_type=F32)


def vmem(shape, dtype):
    return pltpu.VMEM(shape, dtype)


def hbm(shape, dtype):
    return jax.ShapeDtypeStruct(shape, dtype)


def call(
    kernel, out_shapes, place, *args, space=pltpu.VMEM, out_space=pltpu.VMEM, filled=None, scratch=()
):
    args = [pltpu.with_memory_space_constraint(a, space) for a in args]
    specs = [pl.BlockSpec(memory_space=pltpu.SMEM)]
    if filled is not None:
        args = [pltpu.with_memory_space_constraint(filled, pltpu.HBM)] + args
        specs += [pl.BlockSpec(memory_space=pltpu.HBM)]
    specs += [pl.BlockSpec(memory_space=space)] * (len(args) + 1 - len(specs))
    return pl.pallas_call(
        kernel,
        out_shape=out_shapes,
        in_specs=specs,
        out_specs=[pl.BlockSpec(memory_space=out_space) for _ in out_shapes],
        scratch_shapes=scratch,
        input_output_aliases={} if filled is None else {1: 0},
        compiler_params=pltpu.CompilerParams(vmem_limit_bytes=VMEM_BYTES),
    )(place, *args)


def load_kernel(parts, place, q_any, g_any, o_any, k_any, v_any, l_any, *refs):
    q_ref, g_ref, o_ref = refs[:3]
    count = 2 + (parts - 2) // 2
    kv_refs, lse_ref = refs[3 : 3 + count], refs[3 + count]
    k_ref, v_ref, l_ref, sems = refs[4 + count :]
    own = place[0]
    rows = k_ref.shape[0]
    pairs = [(k_any, k_ref), (v_any, v_ref), (l_any, l_ref)]
    pairs += [(q_any, q_ref), (g_any, g_ref), (o_any, o_ref)]
    copies = [
        pltpu.make_async_copy(source, target, sems.at[i])
        for i, (source, target) in enumerate(pairs)
    ]
    for copy in copies:
        copy.start()
    for copy in copies[:3]:
        copy.wait()
    for m in range(parts):
        col = pl.multiple_of((own ^ m) * HEAD_DIM, HEAD_DIM)
        target, first = (kv_refs[m], 0) if m < 2 else (kv_refs[1 + m // 2], m % 2 * 2 * rows)
        target[first : first + rows, :] = k_ref[:, pl.ds(col, HEAD_DIM)]
        target[first + rows : first + 2 * rows, :] = v_ref[:, pl.ds(col, HEAD_DIM)]
    for m in range(parts):
        piece = l_ref[:, :rows]
        for c in range(1, parts):
            piece = jnp.where((own ^ m) == c, l_ref[:, c * rows : (c + 1) * rows], piece)
        piece = piece * math.log2(math.e)
        lse_ref[8 * m : 8 * m + PAIRS, :] = jnp.concatenate([piece[:PAIRS], piece[PAIRS:]], axis=1)
        lse_ref[8 * m + PAIRS : 8 * m + 8, :] = jnp.zeros((8 - PAIRS, 2 * rows), F32)
    for copy in copies[3:]:
        copy.wait()


def pack_kernel(m, place, q_ref, g_ref, o_ref, qg_ref):
    rows = q_ref.shape[0]
    span = GROUP * rows
    base = (place[0] ^ m) * (GROUP * HEAD_DIM)
    lane = lax.broadcasted_iota(jnp.int32, (2 * rows, HEAD_DIM), 1)
    dots = jnp.zeros((2 * rows, HEAD_DIM), F32)
    sums = []
    for i, h in enumerate(HEAD_ORDER):
        col = pl.multiple_of(base + h * HEAD_DIM, HEAD_DIM)
        qg_ref[i * rows : (i + 1) * rows, :] = q_ref[:, pl.ds(col, HEAD_DIM)]
        grad = g_ref[:, pl.ds(col, HEAD_DIM)]
        qg_ref[span + i * rows : span + (i + 1) * rows, :] = grad
        prod = grad.astype(F32) * o_ref[:, pl.ds(col, HEAD_DIM)].astype(F32)
        sums.append(jnp.sum(prod, axis=1, keepdims=True))
    for j in range(PAIRS):
        pair = jnp.concatenate([sums[2 * j], sums[2 * j + 1]], axis=0)
        dots = jnp.where(lane == j, pair, dots)
    full = dots.T[:8, :]
    high = full.astype(BF16).astype(F32)
    mid = (full - high).astype(BF16).astype(F32)
    low = (full - high) - mid
    qg_ref[2 * span :, :] = jnp.concatenate([high, mid, low, jnp.zeros_like(high)], axis=0).astype(
        BF16
    )


def forward_kernel(parts, place, *refs):
    out = refs[-1]
    size = refs[0].shape[0]
    out[:size, :] = refs[0][...]
    for i in range(1, parts // 2):
        out[i * size : (i + 1) * size, :] = refs[i][size:, :]


def join_kernel(parts, place, *refs):
    near, far, passed, out = refs[0], refs[1 : parts // 2], refs[-2], refs[-1]
    rows = out.shape[0] // (2 * parts)
    for m in range(parts):
        if m % 2:
            source, first = passed, m // 2 * 2 * rows
        else:
            source, first = (far[m // 2 - 1], 0) if m else (near, 0)
        out[m * rows : (m + 1) * rows, :] = source[first : first + rows, :]
        out[(parts + m) * rows : (parts + m + 1) * rows, :] = source[
            first + rows : first + 2 * rows, :
        ]


def row_of(stack):
    return jnp.concatenate([stack[j : j + 1, :] for j in range(PAIRS)], axis=1)


def step_kernel(pieces, blocks, span, has_dq, has_acc, dq_done, acc_done, place, *refs):
    refs = list(refs)

    def take(count):
        out = refs[:count]
        del refs[:count]
        return out

    qg_refs = take(len(pieces))
    (lse_ref,) = take(1)
    kv_refs = take(blocks)
    dq_in = take(len(pieces)) if has_dq else None
    acc_in = take(blocks) if has_acc else None
    dq_out = take(len(pieces))
    acc_out = take(blocks)
    scale = 1.0 / math.sqrt(HEAD_DIM)
    block = kv_refs[0].shape[0] // 2
    dk = [acc_in[b][:block, :] if has_acc else None for b in range(blocks)]
    dv = [acc_in[b][block:, :] if has_acc else None for b in range(blocks)]
    for i, m in enumerate(pieces):
        query = qg_refs[i][:span, :]
        grad = qg_refs[i][span : 2 * span, :]
        split = qg_refs[i][2 * span : 2 * span + DOT_ROWS, :].astype(F32)
        dots = row_of((split[:8] + split[8:16]) + split[16:24])
        lse = row_of(lse_ref[8 * m : 8 * m + 8, :])
        dq = dq_in[i][...] if has_dq else None
        for b in range(blocks):
            keys = kv_refs[b][:block, :]
            values = kv_refs[b][block:, :]
            probs = jnp.exp2(dot_nt(keys, query) * (scale * math.log2(math.e)) - lse)
            dprobs = dot_nt(values, grad)
            dscores = (probs * (dprobs - dots)).astype(BF16)
            part_v = dot_nn(probs.astype(BF16), grad)
            part_k = dot_nn(dscores, query)
            part_q = dot_tn(keys, dscores)
            dv[b] = part_v if dv[b] is None else dv[b] + part_v
            dk[b] = part_k if dk[b] is None else dk[b] + part_k
            dq = part_q if dq is None else dq + part_q
        if dq_done:
            dq_out[i][...] = (dq.T * scale).astype(dq_out[i].dtype)
        else:
            dq_out[i][...] = dq
    for b in range(blocks):
        acc_out[b][:block, :] = (dk[b] * scale if acc_done else dk[b]).astype(acc_out[b].dtype)
        acc_out[b][block:, :] = dv[b].astype(acc_out[b].dtype)


def total_kernel(parts, levels, place, *refs):
    terms, near_dq, outs = refs[:levels], refs[levels], refs[levels + 1 :]
    total = terms[0][...]
    for term in terms[1:]:
        total = total + term[...].astype(F32)
    rows = total.shape[0] // (2 * parts)
    for m in range(parts):
        outs[m][:rows, :] = total[m * rows : (m + 1) * rows].astype(outs[m].dtype)
        outs[m][rows : 2 * rows, :] = total[(parts + m) * rows : (parts + m + 1) * rows].astype(
            outs[m].dtype
        )
    outs[1][2 * rows :, :] = near_dq[...]


def put_queries(pieces, sources, place, out, stage, sems):
    rows = out.shape[0]
    width = GROUP * HEAD_DIM
    copies = []
    for slot, (m, source) in enumerate(zip(pieces, sources)):
        for i, h in enumerate(HEAD_ORDER):
            first = source.shape[0] - GROUP * rows + i * rows
            stage[slot, :, h * HEAD_DIM : (h + 1) * HEAD_DIM] = source[
                first : first + rows, :
            ].astype(F32)
        col = pl.multiple_of((place[0] ^ m) * width, width)
        copies.append(
            pltpu.make_async_copy(stage.at[slot], out.at[:, pl.ds(col, width)], sems.at[slot])
        )
        copies[-1].start()
    return copies


def first_kernel(pieces, place, *refs):
    out, stage, sems = refs[-3:]
    for copy in put_queries(pieces, refs[: len(pieces)], place, out, stage, sems):
        copy.wait()


def more_kernel(pieces, place, filled, *refs):
    out, stage, sems = refs[-3:]
    for copy in put_queries(pieces, refs[: len(pieces)], place, out, stage, sems):
        copy.wait()


def finish_kernel(parts, place, filled, *refs):
    pieces, refs = refs[:parts], refs[parts:]
    out, out_k, out_v, stage, stage_k, stage_v, sems = refs
    rows = out.shape[0]
    copies = put_queries((1,), (pieces[1],), place, out, stage, sems)
    for m in range(parts):
        col = pl.multiple_of((place[0] ^ m) * HEAD_DIM, HEAD_DIM)
        stage_k[:, pl.ds(col, HEAD_DIM)] = pieces[m][:rows, :].astype(F32)
        stage_v[:, pl.ds(col, HEAD_DIM)] = pieces[m][rows : 2 * rows, :].astype(F32)
    copies.append(pltpu.make_async_copy(stage_k, out_k, sems.at[1]))
    copies.append(pltpu.make_async_copy(stage_v, out_v, sems.at[2]))
    for copy in copies[1:]:
        copy.start()
    for copy in copies:
        copy.wait()


def swap(value, axis, distance):
    return lax.ppermute(value, axis, [(i, i ^ distance) for i in range(lax.axis_size(axis))])


def far_order(levels):
    return [b for b in (2, 3, 1) if b < levels] + list(range(4, levels))


def on_device(queries, key_rows, value_rows, attn_out, out_grad, logsumexp):
    parts = lax.axis_size("head")
    levels = lax.axis_size("ctx").bit_length()
    rows = queries.shape[0]
    block = rows * parts
    span = rows * GROUP
    place = lax.axis_index("head").astype(jnp.int32).reshape(1)

    *rows_in, lse = call(
        functools.partial(load_kernel, parts),
        [vmem(queries.shape, BF16)] * 3
        + [vmem((2 * rows, HEAD_DIM), BF16)] * 2
        + [vmem((4 * rows, HEAD_DIM), BF16)] * (parts // 2 - 1)
        + [vmem((8 * parts, 2 * rows), F32)],
        place,
        queries,
        out_grad,
        attn_out,
        key_rows,
        value_rows,
        logsumexp,
        space=pltpu.HBM,
        scratch=[
            vmem(key_rows.shape, BF16),
            vmem(value_rows.shape, BF16),
            vmem(logsumexp.shape, F32),
            pltpu.SemaphoreType.DMA((6,)),
        ],
    )
    kv = rows_in[3:]
    qg = []
    for m in range(parts):
        (packed,) = call(
            functools.partial(pack_kernel, m),
            [vmem((2 * span + DOT_ROWS, HEAD_DIM), BF16)],
            place,
            *rows_in[:3],
        )
        qg.append(packed if m == 0 else swap(packed, "head", m))
    kv_far = [swap(kv[1 + i], "head", 2 * i) for i in range(1, parts // 2)]
    (passed,) = call(
        functools.partial(forward_kernel, parts),
        [vmem((parts * rows, HEAD_DIM), BF16)],
        place,
        kv[1],
        *kv_far,
    )
    passed = swap(passed, "head", 1)
    (kv_own,) = call(
        functools.partial(join_kernel, parts),
        [vmem((2 * block, HEAD_DIM), BF16)],
        place,
        kv[0],
        *kv_far,
        passed,
    )
    kv_all = [kv_own] + [swap(kv_own, "ctx", 1 << (b - 1)) for b in range(1, levels)]

    dq = [None] * parts
    acc = [None] * levels

    def step(pieces, blocks, dq_done, acc_done):
        has_dq = dq[pieces[0]] is not None
        has_acc = acc[blocks[0]] is not None
        outs = []
        for m in pieces:
            if dq_done:
                outs.append(vmem((span, HEAD_DIM), F32 if m == 0 else BF16))
            else:
                outs.append(vmem((HEAD_DIM, span), F32))
        for b in blocks:
            outs.append(vmem((2 * block, HEAD_DIM), BF16 if acc_done and b > 0 else F32))
        result = call(
            functools.partial(
                step_kernel, pieces, len(blocks), span, has_dq, has_acc, dq_done, acc_done
            ),
            outs,
            place,
            *[qg[m] for m in pieces],
            lse,
            *[kv_all[b] for b in blocks],
            *([dq[m] for m in pieces] if has_dq else []),
            *([acc[b] for b in blocks] if has_acc else []),
        )
        for i, m in enumerate(pieces):
            dq[m] = result[i]
            if dq_done and m > 1:
                dq[m] = swap(dq[m], "head", m)
        for i, b in enumerate(blocks):
            acc[b] = result[len(pieces) + i]
            if acc_done and b > 0:
                acc[b] = swap(acc[b], "ctx", 1 << (b - 1))

    early = tuple(range(parts - 1))
    step((0,), (0,), False, False)
    step(early[1:], (0,), False, False)
    for b in range(1, levels):
        step(early, (b,), b == levels - 1, False)
    for b in far_order(levels) + [0]:
        step((parts - 1,), (b,), b == 0, True)

    dkv = call(
        functools.partial(total_kernel, parts, levels),
        [
            vmem((2 * rows + (span if m == 1 else 0), HEAD_DIM), F32 if m == 0 else BF16)
            for m in range(parts)
        ],
        place,
        *acc,
        dq[1],
    )
    dkv = [dkv[0]] + [swap(dkv[m], "head", m) for m in range(1, parts)]
    width = GROUP * HEAD_DIM

    def stage(count):
        return vmem((count, rows, width), F32)

    early = (0,) + tuple(range(2, parts - 1))
    (grad_q,) = call(
        functools.partial(first_kernel, early),
        [hbm(queries.shape, F32)],
        place,
        *[dq[m] for m in early],
        out_space=pltpu.HBM,
        scratch=[stage(len(early)), pltpu.SemaphoreType.DMA((len(early),))],
    )
    (grad_q,) = call(
        functools.partial(more_kernel, (parts - 1,)),
        [hbm(queries.shape, F32)],
        place,
        dq[parts - 1],
        out_space=pltpu.HBM,
        filled=grad_q,
        scratch=[stage(1), pltpu.SemaphoreType.DMA((1,))],
    )
    grad_q, grad_k, grad_v = call(
        functools.partial(finish_kernel, parts),
        [hbm(queries.shape, F32), hbm(key_rows.shape, F32), hbm(value_rows.shape, F32)],
        place,
        *dkv,
        out_space=pltpu.HBM,
        filled=grad_q,
        scratch=[
            stage(1),
            vmem(key_rows.shape, F32),
            vmem(value_rows.shape, F32),
            pltpu.SemaphoreType.DMA((3,)),
        ],
    )
    return (grad_q, grad_k, grad_v)


def solution(mesh):
    rows = P(("ctx", "head"), None)
    return jax.shard_map(
        on_device,
        mesh=mesh,
        in_specs=(rows, rows, rows, rows, rows, P("head", "ctx")),
        out_specs=(rows, rows, rows),
        check_vma=False,
    )
```

```python
import functools
import math

import jax
import jax.numpy as jnp
from jax import lax
from jax.experimental import pallas as pl
from jax.experimental.pallas import tpu as pltpu
from jax.sharding import PartitionSpec as P


HEAD_DIM = 128
GROUP = 8
PAIRS = GROUP // 2
DOT_ROWS = 32
VMEM_BYTES = 16 * 1024 * 1024


F32 = jnp.float32
BF16 = jnp.bfloat16

HEAD_ORDER = [j + half * PAIRS for j in range(PAIRS) for half in range(2)]


def dot_nt(a, b):
    return lax.dot_general(a, b, (((1,), (1,)), ((), ())), preferred_element_type=F32)


def dot_nn(a, b):
    return lax.dot_general(a, b, (((1,), (0,)), ((), ())), preferred_element_type=F32)


def dot_tn(a, b):
    return lax.dot_general(a, b, (((0,), (0,)), ((), ())), preferred_element_type=F32)


def vmem(shape, dtype):
    return pltpu.VMEM(shape, dtype)


def hbm(shape, dtype):
    return jax.ShapeDtypeStruct(shape, dtype)


def call(
    kernel, out_shapes, place, *args, space=pltpu.VMEM, out_space=pltpu.VMEM, filled=None, scratch=()
):
    args = [pltpu.with_memory_space_constraint(a, space) for a in args]
    specs = [pl.BlockSpec(memory_space=pltpu.SMEM)]
    if filled is not None:
        args = [pltpu.with_memory_space_constraint(filled, pltpu.HBM)] + args
        specs += [pl.BlockSpec(memory_space=pltpu.HBM)]
    specs += [pl.BlockSpec(memory_space=space)] * (len(args) + 1 - len(specs))
    return pl.pallas_call(
        kernel,
        out_shape=out_shapes,
        in_specs=specs,
        out_specs=[pl.BlockSpec(memory_space=out_space) for _ in out_shapes],
        scratch_shapes=scratch,
        input_output_aliases={} if filled is None else {1: 0},
        compiler_params=pltpu.CompilerParams(vmem_limit_bytes=VMEM_BYTES),
    )(place, *args)


def load_kernel(parts, place, q_any, g_any, o_any, k_any, v_any, l_any, *refs):
    q_ref, g_ref, o_ref = refs[:3]
    kv_refs, lse_ref = refs[3 : 3 + parts], refs[3 + parts]
    k_ref, v_ref, l_ref, sems = refs[4 + parts :]
    own = place[0]
    rows = k_ref.shape[0]
    pairs = [(k_any, k_ref), (v_any, v_ref), (l_any, l_ref)]
    pairs += [(q_any, q_ref), (g_any, g_ref), (o_any, o_ref)]
    copies = [
        pltpu.make_async_copy(source, target, sems.at[i])
        for i, (source, target) in enumerate(pairs)
    ]
    for copy in copies:
        copy.start()
    for copy in copies[:3]:
        copy.wait()
    for m in range(parts):
        col = pl.multiple_of((own ^ m) * HEAD_DIM, HEAD_DIM)
        kv_refs[m][:rows, :] = k_ref[:, pl.ds(col, HEAD_DIM)]
        kv_refs[m][rows:, :] = v_ref[:, pl.ds(col, HEAD_DIM)]
    for m in range(parts):
        piece = l_ref[:, :rows]
        for c in range(1, parts):
            piece = jnp.where((own ^ m) == c, l_ref[:, c * rows : (c + 1) * rows], piece)
        piece = piece * math.log2(math.e)
        lse_ref[8 * m : 8 * m + PAIRS, :] = jnp.concatenate([piece[:PAIRS], piece[PAIRS:]], axis=1)
        lse_ref[8 * m + PAIRS : 8 * m + 8, :] = jnp.zeros((8 - PAIRS, 2 * rows), F32)
    for copy in copies[3:]:
        copy.wait()


def pack_kernel(m, place, q_ref, g_ref, o_ref, qg_ref):
    rows = q_ref.shape[0]
    span = GROUP * rows
    base = (place[0] ^ m) * (GROUP * HEAD_DIM)
    lane = lax.broadcasted_iota(jnp.int32, (2 * rows, HEAD_DIM), 1)
    dots = jnp.zeros((2 * rows, HEAD_DIM), F32)
    sums = []
    for i, h in enumerate(HEAD_ORDER):
        col = pl.multiple_of(base + h * HEAD_DIM, HEAD_DIM)
        qg_ref[i * rows : (i + 1) * rows, :] = q_ref[:, pl.ds(col, HEAD_DIM)]
        grad = g_ref[:, pl.ds(col, HEAD_DIM)]
        qg_ref[span + i * rows : span + (i + 1) * rows, :] = grad
        prod = grad.astype(F32) * o_ref[:, pl.ds(col, HEAD_DIM)].astype(F32)
        sums.append(jnp.sum(prod, axis=1, keepdims=True))
    for j in range(PAIRS):
        pair = jnp.concatenate([sums[2 * j], sums[2 * j + 1]], axis=0)
        dots = jnp.where(lane == j, pair, dots)
    full = dots.T[:8, :]
    high = full.astype(BF16).astype(F32)
    mid = (full - high).astype(BF16).astype(F32)
    low = (full - high) - mid
    qg_ref[2 * span :, :] = jnp.concatenate([high, mid, low, jnp.zeros_like(high)], axis=0).astype(
        BF16
    )


def join_kernel(parts, place, *refs):
    pieces, out = refs[:parts], refs[parts]
    rows = out.shape[0] // (2 * parts)
    for m in range(parts):
        out[m * rows : (m + 1) * rows, :] = pieces[m][:rows, :]
        out[(parts + m) * rows : (parts + m + 1) * rows, :] = pieces[m][rows:, :]


def row_of(stack):
    return jnp.concatenate([stack[j : j + 1, :] for j in range(PAIRS)], axis=1)


def step_kernel(pieces, blocks, span, has_dq, has_acc, dq_done, acc_done, place, *refs):
    refs = list(refs)

    def take(count):
        out = refs[:count]
        del refs[:count]
        return out

    qg_refs = take(len(pieces))
    (lse_ref,) = take(1)
    kv_refs = take(blocks)
    dq_in = take(len(pieces)) if has_dq else None
    acc_in = take(blocks) if has_acc else None
    dq_out = take(len(pieces))
    acc_out = take(blocks)
    scale = 1.0 / math.sqrt(HEAD_DIM)
    block = kv_refs[0].shape[0] // 2
    dk = [acc_in[b][:block, :] if has_acc else None for b in range(blocks)]
    dv = [acc_in[b][block:, :] if has_acc else None for b in range(blocks)]
    for i, m in enumerate(pieces):
        query = qg_refs[i][:span, :]
        grad = qg_refs[i][span : 2 * span, :]
        split = qg_refs[i][2 * span : 2 * span + DOT_ROWS, :].astype(F32)
        dots = row_of((split[:8] + split[8:16]) + split[16:24])
        lse = row_of(lse_ref[8 * m : 8 * m + 8, :])
        dq = dq_in[i][...] if has_dq else None
        for b in range(blocks):
            keys = kv_refs[b][:block, :]
            values = kv_refs[b][block:, :]
            probs = jnp.exp2(dot_nt(keys, query) * (scale * math.log2(math.e)) - lse)
            dprobs = dot_nt(values, grad)
            dscores = (probs * (dprobs - dots)).astype(BF16)
            part_v = dot_nn(probs.astype(BF16), grad)
            part_k = dot_nn(dscores, query)
            part_q = dot_tn(keys, dscores)
            dv[b] = part_v if dv[b] is None else dv[b] + part_v
            dk[b] = part_k if dk[b] is None else dk[b] + part_k
            dq = part_q if dq is None else dq + part_q
        if dq_done:
            dq_out[i][...] = (dq.T * scale).astype(dq_out[i].dtype)
        else:
            dq_out[i][...] = dq
    for b in range(blocks):
        acc_out[b][:block, :] = (dk[b] * scale if acc_done else dk[b]).astype(acc_out[b].dtype)
        acc_out[b][block:, :] = dv[b].astype(acc_out[b].dtype)


def total_kernel(parts, levels, place, *refs):
    terms, near_dq, outs = refs[:levels], refs[levels], refs[levels + 1 :]
    total = terms[0][...]
    for term in terms[1:]:
        total = total + term[...].astype(F32)
    rows = total.shape[0] // (2 * parts)
    for m in range(parts):
        outs[m][:rows, :] = total[m * rows : (m + 1) * rows].astype(outs[m].dtype)
        outs[m][rows : 2 * rows, :] = total[(parts + m) * rows : (parts + m + 1) * rows].astype(
            outs[m].dtype
        )
    outs[1][2 * rows :, :] = near_dq[...]


def put_queries(pieces, sources, place, out, stage, sems):
    rows = out.shape[0]
    width = GROUP * HEAD_DIM
    copies = []
    for slot, (m, source) in enumerate(zip(pieces, sources)):
        for i, h in enumerate(HEAD_ORDER):
            first = source.shape[0] - GROUP * rows + i * rows
            stage[slot, :, h * HEAD_DIM : (h + 1) * HEAD_DIM] = source[
                first : first + rows, :
            ].astype(F32)
        col = pl.multiple_of((place[0] ^ m) * width, width)
        copies.append(
            pltpu.make_async_copy(stage.at[slot], out.at[:, pl.ds(col, width)], sems.at[slot])
        )
        copies[-1].start()
    return copies


def first_kernel(pieces, place, *refs):
    out, stage, sems = refs[-3:]
    for copy in put_queries(pieces, refs[: len(pieces)], place, out, stage, sems):
        copy.wait()


def more_kernel(pieces, place, filled, *refs):
    out, stage, sems = refs[-3:]
    for copy in put_queries(pieces, refs[: len(pieces)], place, out, stage, sems):
        copy.wait()


def finish_kernel(parts, place, filled, *refs):
    pieces, refs = refs[:parts], refs[parts:]
    out, out_k, out_v, stage, stage_k, stage_v, sems = refs
    rows = out.shape[0]
    copies = put_queries((1,), (pieces[1],), place, out, stage, sems)
    for m in range(parts):
        col = pl.multiple_of((place[0] ^ m) * HEAD_DIM, HEAD_DIM)
        stage_k[:, pl.ds(col, HEAD_DIM)] = pieces[m][:rows, :].astype(F32)
        stage_v[:, pl.ds(col, HEAD_DIM)] = pieces[m][rows : 2 * rows, :].astype(F32)
    copies.append(pltpu.make_async_copy(stage_k, out_k, sems.at[1]))
    copies.append(pltpu.make_async_copy(stage_v, out_v, sems.at[2]))
    for copy in copies[1:]:
        copy.start()
    for copy in copies:
        copy.wait()


def swap(value, axis, distance):
    return lax.ppermute(value, axis, [(i, i ^ distance) for i in range(lax.axis_size(axis))])


def far_order(levels):
    return [b for b in (2, 3, 1) if b < levels] + list(range(4, levels))


def use_order(levels):
    return [b for b in (2, 1, 3) if b < levels] + list(range(4, levels))


def on_device(queries, key_rows, value_rows, attn_out, out_grad, logsumexp):
    parts = lax.axis_size("head")
    levels = lax.axis_size("ctx").bit_length()
    rows = queries.shape[0]
    block = rows * parts
    span = rows * GROUP
    place = lax.axis_index("head").astype(jnp.int32).reshape(1)

    *rows_in, lse = call(
        functools.partial(load_kernel, parts),
        [vmem(queries.shape, BF16)] * 3
        + [vmem((2 * rows, HEAD_DIM), BF16)] * parts
        + [vmem((8 * parts, 2 * rows), F32)],
        place,
        queries,
        out_grad,
        attn_out,
        key_rows,
        value_rows,
        logsumexp,
        space=pltpu.HBM,
        scratch=[
            vmem(key_rows.shape, BF16),
            vmem(value_rows.shape, BF16),
            vmem(logsumexp.shape, F32),
            pltpu.SemaphoreType.DMA((6,)),
        ],
    )
    kv = rows_in[3:]
    qg = []
    for m in range(parts):
        (packed,) = call(
            functools.partial(pack_kernel, m),
            [vmem((2 * span + DOT_ROWS, HEAD_DIM), BF16)],
            place,
            *rows_in[:3],
        )
        qg.append(packed if m == 0 else swap(packed, "head", m))
    kv = [kv[0]] + [swap(kv[m], "head", m) for m in range(1, parts)]
    (kv_own,) = call(
        functools.partial(join_kernel, parts), [vmem((2 * block, HEAD_DIM), BF16)], place, *kv
    )
    kv_all = [kv_own] + [swap(kv_own, "ctx", 1 << (b - 1)) for b in range(1, levels)]

    dq = [None] * parts
    acc = [None] * levels

    def step(pieces, blocks, dq_done, acc_done):
        has_dq = dq[pieces[0]] is not None
        has_acc = acc[blocks[0]] is not None
        outs = []
        for m in pieces:
            if dq_done:
                outs.append(vmem((span, HEAD_DIM), F32 if m == 0 else BF16))
            else:
                outs.append(vmem((HEAD_DIM, span), F32))
        for b in blocks:
            outs.append(vmem((2 * block, HEAD_DIM), BF16 if acc_done and b > 0 else F32))
        result = call(
            functools.partial(
                step_kernel, pieces, len(blocks), span, has_dq, has_acc, dq_done, acc_done
            ),
            outs,
            place,
            *[qg[m] for m in pieces],
            lse,
            *[kv_all[b] for b in blocks],
            *([dq[m] for m in pieces] if has_dq else []),
            *([acc[b] for b in blocks] if has_acc else []),
        )
        for i, m in enumerate(pieces):
            dq[m] = result[i]
            if dq_done and m > 1:
                dq[m] = swap(dq[m], "head", m)
        for i, b in enumerate(blocks):
            acc[b] = result[len(pieces) + i]
            if acc_done and b > 0:
                acc[b] = swap(acc[b], "ctx", 1 << (b - 1))

    early = tuple(range(parts - 1))
    step((0,), (0,), False, False)
    step(early[1:], (0,), False, False)
    for b in use_order(levels):
        step(early, (b,), b == use_order(levels)[-1], False)
    for b in far_order(levels) + [0]:
        step((parts - 1,), (b,), b == 0, True)

    dkv = call(
        functools.partial(total_kernel, parts, levels),
        [
            vmem((2 * rows + (span if m == 1 else 0), HEAD_DIM), F32 if m == 0 else BF16)
            for m in range(parts)
        ],
        place,
        *acc,
        dq[1],
    )
    dkv = [dkv[0]] + [swap(dkv[m], "head", m) for m in range(1, parts)]
    width = GROUP * HEAD_DIM

    def stage(count):
        return vmem((count, rows, width), F32)

    early = (0,) + tuple(range(2, parts - 1))
    (grad_q,) = call(
        functools.partial(first_kernel, early),
        [hbm(queries.shape, F32)],
        place,
        *[dq[m] for m in early],
        out_space=pltpu.HBM,
        scratch=[stage(len(early)), pltpu.SemaphoreType.DMA((len(early),))],
    )
    (grad_q,) = call(
        functools.partial(more_kernel, (parts - 1,)),
        [hbm(queries.shape, F32)],
        place,
        dq[parts - 1],
        out_space=pltpu.HBM,
        filled=grad_q,
        scratch=[stage(1), pltpu.SemaphoreType.DMA((1,))],
    )
    grad_q, grad_k, grad_v = call(
        functools.partial(finish_kernel, parts),
        [hbm(queries.shape, F32), hbm(key_rows.shape, F32), hbm(value_rows.shape, F32)],
        place,
        *dkv,
        out_space=pltpu.HBM,
        filled=grad_q,
        scratch=[
            stage(1),
            vmem(key_rows.shape, F32),
            vmem(value_rows.shape, F32),
            pltpu.SemaphoreType.DMA((3,)),
        ],
    )
    return (grad_q, grad_k, grad_v)


def solution(mesh):
    rows = P(("ctx", "head"), None)
    return jax.shard_map(
        on_device,
        mesh=mesh,
        in_specs=(rows, rows, rows, rows, rows, P("head", "ctx")),
        out_specs=(rows, rows, rows),
        check_vma=False,
    )
```

```python
import functools
import math

import jax
import jax.numpy as jnp
from jax import lax
from jax.experimental import pallas as pl
from jax.experimental.pallas import tpu as pltpu
from jax.sharding import PartitionSpec as P


HEAD_DIM = 128
GROUP = 8
PAIRS = GROUP // 2
DOT_ROWS = 32
VMEM_BYTES = 16 * 1024 * 1024


F32 = jnp.float32
BF16 = jnp.bfloat16

HEAD_ORDER = [j + half * PAIRS for j in range(PAIRS) for half in range(2)]


def dot_nt(a, b):
    return lax.dot_general(a, b, (((1,), (1,)), ((), ())), preferred_element_type=F32)


def dot_nn(a, b):
    return lax.dot_general(a, b, (((1,), (0,)), ((), ())), preferred_element_type=F32)


def dot_tn(a, b):
    return lax.dot_general(a, b, (((0,), (0,)), ((), ())), preferred_element_type=F32)


def vmem(shape, dtype):
    return pltpu.VMEM(shape, dtype)


def hbm(shape, dtype):
    return jax.ShapeDtypeStruct(shape, dtype)


def call(
    kernel, out_shapes, place, *args, space=pltpu.VMEM, out_space=pltpu.VMEM, filled=None, scratch=()
):
    args = [pltpu.with_memory_space_constraint(a, space) for a in args]
    specs = [pl.BlockSpec(memory_space=pltpu.SMEM)]
    if filled is not None:
        args = [pltpu.with_memory_space_constraint(filled, pltpu.HBM)] + args
        specs += [pl.BlockSpec(memory_space=pltpu.HBM)]
    specs += [pl.BlockSpec(memory_space=space)] * (len(args) + 1 - len(specs))
    return pl.pallas_call(
        kernel,
        out_shape=out_shapes,
        in_specs=specs,
        out_specs=[pl.BlockSpec(memory_space=out_space) for _ in out_shapes],
        scratch_shapes=scratch,
        input_output_aliases={} if filled is None else {1: 0},
        compiler_params=pltpu.CompilerParams(vmem_limit_bytes=VMEM_BYTES),
    )(place, *args)


def load_kernel(parts, place, q_any, g_any, o_any, k_any, v_any, l_any, *refs):
    q_ref, g_ref, o_ref = refs[:3]
    kv_refs, lse_ref = refs[3 : 3 + parts], refs[3 + parts]
    k_ref, v_ref, l_ref, sems = refs[4 + parts :]
    own = place[0]
    rows = k_ref.shape[0]
    pairs = [(k_any, k_ref), (v_any, v_ref), (l_any, l_ref)]
    pairs += [(q_any, q_ref), (g_any, g_ref), (o_any, o_ref)]
    copies = [
        pltpu.make_async_copy(source, target, sems.at[i])
        for i, (source, target) in enumerate(pairs)
    ]
    for copy in copies:
        copy.start()
    for copy in copies[:3]:
        copy.wait()
    for m in range(parts):
        col = pl.multiple_of((own ^ m) * HEAD_DIM, HEAD_DIM)
        kv_refs[m][:rows, :] = k_ref[:, pl.ds(col, HEAD_DIM)]
        kv_refs[m][rows:, :] = v_ref[:, pl.ds(col, HEAD_DIM)]
    for m in range(parts):
        piece = l_ref[:, :rows]
        for c in range(1, parts):
            piece = jnp.where((own ^ m) == c, l_ref[:, c * rows : (c + 1) * rows], piece)
        piece = piece * math.log2(math.e)
        lse_ref[8 * m : 8 * m + PAIRS, :] = jnp.concatenate([piece[:PAIRS], piece[PAIRS:]], axis=1)
        lse_ref[8 * m + PAIRS : 8 * m + 8, :] = jnp.zeros((8 - PAIRS, 2 * rows), F32)
    for copy in copies[3:]:
        copy.wait()


def pack_kernel(m, place, q_ref, g_ref, o_ref, qg_ref):
    rows = q_ref.shape[0]
    span = GROUP * rows
    base = (place[0] ^ m) * (GROUP * HEAD_DIM)
    lane = lax.broadcasted_iota(jnp.int32, (2 * rows, HEAD_DIM), 1)
    dots = jnp.zeros((2 * rows, HEAD_DIM), F32)
    sums = []
    for i, h in enumerate(HEAD_ORDER):
        col = pl.multiple_of(base + h * HEAD_DIM, HEAD_DIM)
        qg_ref[i * rows : (i + 1) * rows, :] = q_ref[:, pl.ds(col, HEAD_DIM)]
        grad = g_ref[:, pl.ds(col, HEAD_DIM)]
        qg_ref[span + i * rows : span + (i + 1) * rows, :] = grad
        prod = grad.astype(F32) * o_ref[:, pl.ds(col, HEAD_DIM)].astype(F32)
        sums.append(jnp.sum(prod, axis=1, keepdims=True))
    for j in range(PAIRS):
        pair = jnp.concatenate([sums[2 * j], sums[2 * j + 1]], axis=0)
        dots = jnp.where(lane == j, pair, dots)
    full = dots.T[:8, :]
    high = full.astype(BF16).astype(F32)
    mid = (full - high).astype(BF16).astype(F32)
    low = (full - high) - mid
    qg_ref[2 * span :, :] = jnp.concatenate([high, mid, low, jnp.zeros_like(high)], axis=0).astype(
        BF16
    )


def join_kernel(parts, place, *refs):
    pieces, out = refs[:parts], refs[parts]
    rows = out.shape[0] // (2 * parts)
    for m in range(parts):
        out[m * rows : (m + 1) * rows, :] = pieces[m][:rows, :]
        out[(parts + m) * rows : (parts + m + 1) * rows, :] = pieces[m][rows:, :]


def row_of(stack):
    return jnp.concatenate([stack[j : j + 1, :] for j in range(PAIRS)], axis=1)


def step_kernel(pieces, blocks, span, has_dq, has_acc, dq_done, acc_done, place, *refs):
    refs = list(refs)

    def take(count):
        out = refs[:count]
        del refs[:count]
        return out

    qg_refs = take(len(pieces))
    (lse_ref,) = take(1)
    kv_refs = take(blocks)
    dq_in = take(len(pieces)) if has_dq else None
    acc_in = take(blocks) if has_acc else None
    dq_out = take(len(pieces))
    acc_out = take(blocks)
    scale = 1.0 / math.sqrt(HEAD_DIM)
    block = kv_refs[0].shape[0] // 2
    dk = [acc_in[b][:block, :] if has_acc else None for b in range(blocks)]
    dv = [acc_in[b][block:, :] if has_acc else None for b in range(blocks)]
    for i, m in enumerate(pieces):
        query = qg_refs[i][:span, :]
        grad = qg_refs[i][span : 2 * span, :]
        split = qg_refs[i][2 * span : 2 * span + DOT_ROWS, :].astype(F32)
        dots = row_of((split[:8] + split[8:16]) + split[16:24])
        lse = row_of(lse_ref[8 * m : 8 * m + 8, :])
        dq = dq_in[i][...] if has_dq else None
        for b in range(blocks):
            keys = kv_refs[b][:block, :]
            values = kv_refs[b][block:, :]
            probs = jnp.exp2(dot_nt(keys, query) * (scale * math.log2(math.e)) - lse)
            dprobs = dot_nt(values, grad)
            dscores = (probs * (dprobs - dots)).astype(BF16)
            part_v = dot_nn(probs.astype(BF16), grad)
            part_k = dot_nn(dscores, query)
            part_q = dot_tn(keys, dscores)
            dv[b] = part_v if dv[b] is None else dv[b] + part_v
            dk[b] = part_k if dk[b] is None else dk[b] + part_k
            dq = part_q if dq is None else dq + part_q
        if dq_done:
            dq_out[i][...] = (dq.T * scale).astype(dq_out[i].dtype)
        else:
            dq_out[i][...] = dq
    for b in range(blocks):
        acc_out[b][:block, :] = (dk[b] * scale if acc_done else dk[b]).astype(acc_out[b].dtype)
        acc_out[b][block:, :] = dv[b].astype(acc_out[b].dtype)


def total_kernel(parts, levels, place, *refs):
    terms, near_dq, outs = refs[:levels], refs[levels], refs[levels + 1 :]
    total = terms[0][...]
    for term in terms[1:]:
        total = total + term[...].astype(F32)
    rows = total.shape[0] // (2 * parts)
    for m in range(parts):
        outs[m][:rows, :] = total[m * rows : (m + 1) * rows].astype(outs[m].dtype)
        outs[m][rows : 2 * rows, :] = total[(parts + m) * rows : (parts + m + 1) * rows].astype(
            outs[m].dtype
        )
    outs[1][2 * rows :, :] = near_dq[...]


def put_queries(pieces, sources, place, out, stage, sems):
    rows = out.shape[0]
    width = GROUP * HEAD_DIM
    copies = []
    for slot, (m, source) in enumerate(zip(pieces, sources)):
        for i, h in enumerate(HEAD_ORDER):
            first = source.shape[0] - GROUP * rows + i * rows
            stage[slot, :, h * HEAD_DIM : (h + 1) * HEAD_DIM] = source[
                first : first + rows, :
            ].astype(F32)
        col = pl.multiple_of((place[0] ^ m) * width, width)
        copies.append(
            pltpu.make_async_copy(stage.at[slot], out.at[:, pl.ds(col, width)], sems.at[slot])
        )
        copies[-1].start()
    return copies


def first_kernel(pieces, place, *refs):
    out, stage, sems = refs[-3:]
    for copy in put_queries(pieces, refs[: len(pieces)], place, out, stage, sems):
        copy.wait()


def more_kernel(pieces, place, filled, *refs):
    out, stage, sems = refs[-3:]
    for copy in put_queries(pieces, refs[: len(pieces)], place, out, stage, sems):
        copy.wait()


def finish_kernel(parts, place, filled, *refs):
    pieces, refs = refs[:parts], refs[parts:]
    out, out_k, out_v, stage, stage_k, stage_v, sems = refs
    rows = out.shape[0]
    copies = put_queries((1,), (pieces[1],), place, out, stage, sems)
    for m in range(parts):
        col = pl.multiple_of((place[0] ^ m) * HEAD_DIM, HEAD_DIM)
        stage_k[:, pl.ds(col, HEAD_DIM)] = pieces[m][:rows, :].astype(F32)
        stage_v[:, pl.ds(col, HEAD_DIM)] = pieces[m][rows : 2 * rows, :].astype(F32)
    copies.append(pltpu.make_async_copy(stage_k, out_k, sems.at[1]))
    copies.append(pltpu.make_async_copy(stage_v, out_v, sems.at[2]))
    for copy in copies[1:]:
        copy.start()
    for copy in copies:
        copy.wait()


def swap(value, axis, distance):
    return lax.ppermute(value, axis, [(i, i ^ distance) for i in range(lax.axis_size(axis))])


def far_order(levels):
    return [b for b in (2, 3, 1) if b < levels] + list(range(4, levels))


def use_order(levels):
    return [b for b in (2, 1, 3) if b < levels] + list(range(4, levels))


def on_device(queries, key_rows, value_rows, attn_out, out_grad, logsumexp):
    parts = lax.axis_size("head")
    levels = lax.axis_size("ctx").bit_length()
    rows = queries.shape[0]
    block = rows * parts
    span = rows * GROUP
    place = lax.axis_index("head").astype(jnp.int32).reshape(1)

    *rows_in, lse = call(
        functools.partial(load_kernel, parts),
        [vmem(queries.shape, BF16)] * 3
        + [vmem((2 * rows, HEAD_DIM), BF16)] * parts
        + [vmem((8 * parts, 2 * rows), F32)],
        place,
        queries,
        out_grad,
        attn_out,
        key_rows,
        value_rows,
        logsumexp,
        space=pltpu.HBM,
        scratch=[
            vmem(key_rows.shape, BF16),
            vmem(value_rows.shape, BF16),
            vmem(logsumexp.shape, F32),
            pltpu.SemaphoreType.DMA((6,)),
        ],
    )
    kv = rows_in[3:]
    qg = []
    for m in range(parts):
        (packed,) = call(
            functools.partial(pack_kernel, m),
            [vmem((2 * span + DOT_ROWS, HEAD_DIM), BF16)],
            place,
            *rows_in[:3],
        )
        qg.append(packed if m == 0 else swap(packed, "head", m))
    kv = [kv[0]] + [swap(kv[m], "head", m) for m in range(1, parts)]
    (kv_own,) = call(
        functools.partial(join_kernel, parts), [vmem((2 * block, HEAD_DIM), BF16)], place, *kv
    )
    kv_all = [kv_own] + [swap(kv_own, "ctx", 1 << (b - 1)) for b in range(1, levels)]

    dq = [None] * parts
    acc = [None] * levels

    def step(pieces, blocks, dq_done, acc_done):
        has_dq = dq[pieces[0]] is not None
        has_acc = acc[blocks[0]] is not None
        outs = []
        for m in pieces:
            if dq_done:
                outs.append(vmem((span, HEAD_DIM), F32 if m == 0 else BF16))
            else:
                outs.append(vmem((HEAD_DIM, span), F32))
        for b in blocks:
            outs.append(vmem((2 * block, HEAD_DIM), BF16 if acc_done and b > 0 else F32))
        result = call(
            functools.partial(
                step_kernel, pieces, len(blocks), span, has_dq, has_acc, dq_done, acc_done
            ),
            outs,
            place,
            *[qg[m] for m in pieces],
            lse,
            *[kv_all[b] for b in blocks],
            *([dq[m] for m in pieces] if has_dq else []),
            *([acc[b] for b in blocks] if has_acc else []),
        )
        for i, m in enumerate(pieces):
            dq[m] = result[i]
            if dq_done and m > 1:
                dq[m] = swap(dq[m], "head", m)
        for i, b in enumerate(blocks):
            acc[b] = result[len(pieces) + i]
            if acc_done and b > 0:
                acc[b] = swap(acc[b], "ctx", 1 << (b - 1))

    early = tuple(range(parts - 1))
    hops = use_order(levels)
    step((0,), (0,), False, False)
    step((1,), (0,), False, False)
    for b in hops[:-1]:
        step((0, 1), (b,), False, False)
    step(early[2:], (0, *hops[:-1]), False, False)
    step(early, (hops[-1],), True, False)
    for b in far_order(levels) + [0]:
        step((parts - 1,), (b,), b == 0, True)

    dkv = call(
        functools.partial(total_kernel, parts, levels),
        [
            vmem((2 * rows + (span if m == 1 else 0), HEAD_DIM), F32 if m == 0 else BF16)
            for m in range(parts)
        ],
        place,
        *acc,
        dq[1],
    )
    dkv = [dkv[0]] + [swap(dkv[m], "head", m) for m in range(1, parts)]
    width = GROUP * HEAD_DIM

    def stage(count):
        return vmem((count, rows, width), F32)

    early = (0,) + tuple(range(2, parts - 1))
    (grad_q,) = call(
        functools.partial(first_kernel, early),
        [hbm(queries.shape, F32)],
        place,
        *[dq[m] for m in early],
        out_space=pltpu.HBM,
        scratch=[stage(len(early)), pltpu.SemaphoreType.DMA((len(early),))],
    )
    (grad_q,) = call(
        functools.partial(more_kernel, (parts - 1,)),
        [hbm(queries.shape, F32)],
        place,
        dq[parts - 1],
        out_space=pltpu.HBM,
        filled=grad_q,
        scratch=[stage(1), pltpu.SemaphoreType.DMA((1,))],
    )
    grad_q, grad_k, grad_v = call(
        functools.partial(finish_kernel, parts),
        [hbm(queries.shape, F32), hbm(key_rows.shape, F32), hbm(value_rows.shape, F32)],
        place,
        *dkv,
        out_space=pltpu.HBM,
        filled=grad_q,
        scratch=[
            stage(1),
            vmem(key_rows.shape, F32),
            vmem(value_rows.shape, F32),
            pltpu.SemaphoreType.DMA((3,)),
        ],
    )
    return (grad_q, grad_k, grad_v)


def solution(mesh):
    rows = P(("ctx", "head"), None)
    return jax.shard_map(
        on_device,
        mesh=mesh,
        in_specs=(rows, rows, rows, rows, rows, P("head", "ctx")),
        out_specs=(rows, rows, rows),
        check_vma=False,
    )
```

```python
import functools
import math

import jax
import jax.numpy as jnp
from jax import lax
from jax.experimental import pallas as pl
from jax.experimental.pallas import tpu as pltpu
from jax.sharding import PartitionSpec as P


HEAD_DIM = 128
GROUP = 8
PAIRS = GROUP // 2
DOT_ROWS = 32
VMEM_BYTES = 16 * 1024 * 1024


F32 = jnp.float32
BF16 = jnp.bfloat16

HEAD_ORDER = [j + half * PAIRS for j in range(PAIRS) for half in range(2)]


def dot_nt(a, b):
    return lax.dot_general(a, b, (((1,), (1,)), ((), ())), preferred_element_type=F32)


def dot_nn(a, b):
    return lax.dot_general(a, b, (((1,), (0,)), ((), ())), preferred_element_type=F32)


def dot_tn(a, b):
    return lax.dot_general(a, b, (((0,), (0,)), ((), ())), preferred_element_type=F32)


def vmem(shape, dtype):
    return pltpu.VMEM(shape, dtype)


def hbm(shape, dtype):
    return jax.ShapeDtypeStruct(shape, dtype)


def call(
    kernel, out_shapes, place, *args, space=pltpu.VMEM, out_space=pltpu.VMEM, filled=None, scratch=()
):
    args = [pltpu.with_memory_space_constraint(a, space) for a in args]
    specs = [pl.BlockSpec(memory_space=pltpu.SMEM)]
    if filled is not None:
        args = [pltpu.with_memory_space_constraint(filled, pltpu.HBM)] + args
        specs += [pl.BlockSpec(memory_space=pltpu.HBM)]
    specs += [pl.BlockSpec(memory_space=space)] * (len(args) + 1 - len(specs))
    return pl.pallas_call(
        kernel,
        out_shape=out_shapes,
        in_specs=specs,
        out_specs=[pl.BlockSpec(memory_space=out_space) for _ in out_shapes],
        scratch_shapes=scratch,
        input_output_aliases={} if filled is None else {1: 0},
        compiler_params=pltpu.CompilerParams(vmem_limit_bytes=VMEM_BYTES),
    )(place, *args)


def load_kernel(parts, place, q_any, g_any, o_any, k_any, v_any, l_any, *refs):
    q_ref, g_ref, o_ref = refs[:3]
    kv_refs, lse_ref = refs[3 : 3 + parts], refs[3 + parts]
    k_ref, v_ref, l_ref, sems = refs[4 + parts :]
    own = place[0]
    rows = k_ref.shape[0]
    pairs = [(k_any, k_ref), (v_any, v_ref), (l_any, l_ref)]
    pairs += [(q_any, q_ref), (g_any, g_ref), (o_any, o_ref)]
    copies = [
        pltpu.make_async_copy(source, target, sems.at[i])
        for i, (source, target) in enumerate(pairs)
    ]
    for copy in copies:
        copy.start()
    for copy in copies[:3]:
        copy.wait()
    for m in range(parts):
        col = pl.multiple_of((own ^ m) * HEAD_DIM, HEAD_DIM)
        kv_refs[m][:rows, :] = k_ref[:, pl.ds(col, HEAD_DIM)]
        kv_refs[m][rows:, :] = v_ref[:, pl.ds(col, HEAD_DIM)]
    for m in range(parts):
        piece = l_ref[:, :rows]
        for c in range(1, parts):
            piece = jnp.where((own ^ m) == c, l_ref[:, c * rows : (c + 1) * rows], piece)
        piece = piece * math.log2(math.e)
        lse_ref[8 * m : 8 * m + PAIRS, :] = jnp.concatenate([piece[:PAIRS], piece[PAIRS:]], axis=1)
        lse_ref[8 * m + PAIRS : 8 * m + 8, :] = jnp.zeros((8 - PAIRS, 2 * rows), F32)
    for copy in copies[3:]:
        copy.wait()


def pack_kernel(m, place, q_ref, g_ref, o_ref, qg_ref):
    rows = q_ref.shape[0]
    span = GROUP * rows
    base = (place[0] ^ m) * (GROUP * HEAD_DIM)
    lane = lax.broadcasted_iota(jnp.int32, (2 * rows, HEAD_DIM), 1)
    dots = jnp.zeros((2 * rows, HEAD_DIM), F32)
    sums = []
    for i, h in enumerate(HEAD_ORDER):
        col = pl.multiple_of(base + h * HEAD_DIM, HEAD_DIM)
        qg_ref[i * rows : (i + 1) * rows, :] = q_ref[:, pl.ds(col, HEAD_DIM)]
        grad = g_ref[:, pl.ds(col, HEAD_DIM)]
        qg_ref[span + i * rows : span + (i + 1) * rows, :] = grad
        prod = grad.astype(F32) * o_ref[:, pl.ds(col, HEAD_DIM)].astype(F32)
        sums.append(jnp.sum(prod, axis=1, keepdims=True))
    for j in range(PAIRS):
        pair = jnp.concatenate([sums[2 * j], sums[2 * j + 1]], axis=0)
        dots = jnp.where(lane == j, pair, dots)
    full = dots.T[:8, :]
    high = full.astype(BF16).astype(F32)
    mid = (full - high).astype(BF16).astype(F32)
    low = (full - high) - mid
    qg_ref[2 * span :, :] = jnp.concatenate([high, mid, low, jnp.zeros_like(high)], axis=0).astype(
        BF16
    )


def join_kernel(parts, place, *refs):
    pieces, out = refs[:parts], refs[parts]
    rows = out.shape[0] // (2 * parts)
    for m in range(parts):
        out[m * rows : (m + 1) * rows, :] = pieces[m][:rows, :]
        out[(parts + m) * rows : (parts + m + 1) * rows, :] = pieces[m][rows:, :]


def row_of(stack):
    return jnp.concatenate([stack[j : j + 1, :] for j in range(PAIRS)], axis=1)


def step_kernel(pieces, blocks, span, has_dq, has_acc, dq_done, acc_done, place, *refs):
    refs = list(refs)

    def take(count):
        out = refs[:count]
        del refs[:count]
        return out

    qg_refs = take(len(pieces))
    (lse_ref,) = take(1)
    kv_refs = take(blocks)
    dq_in = take(len(pieces)) if has_dq else None
    acc_in = take(blocks) if has_acc else None
    dq_out = take(len(pieces))
    acc_out = take(blocks)
    scale = 1.0 / math.sqrt(HEAD_DIM)
    block = kv_refs[0].shape[0] // 2
    dk = [acc_in[b][:block, :] if has_acc else None for b in range(blocks)]
    dv = [acc_in[b][block:, :] if has_acc else None for b in range(blocks)]
    for i, m in enumerate(pieces):
        query = qg_refs[i][:span, :]
        grad = qg_refs[i][span : 2 * span, :]
        split = qg_refs[i][2 * span : 2 * span + DOT_ROWS, :].astype(F32)
        dots = row_of((split[:8] + split[8:16]) + split[16:24])
        lse = row_of(lse_ref[8 * m : 8 * m + 8, :])
        dq = dq_in[i][...] if has_dq else None
        for b in range(blocks):
            keys = kv_refs[b][:block, :]
            values = kv_refs[b][block:, :]
            probs = jnp.exp2(dot_nt(keys, query) * (scale * math.log2(math.e)) - lse)
            dprobs = dot_nt(values, grad)
            dscores = (probs * (dprobs - dots)).astype(BF16)
            part_v = dot_nn(probs.astype(BF16), grad)
            part_k = dot_nn(dscores, query)
            part_q = dot_tn(keys, dscores)
            dv[b] = part_v if dv[b] is None else dv[b] + part_v
            dk[b] = part_k if dk[b] is None else dk[b] + part_k
            dq = part_q if dq is None else dq + part_q
        if dq_done:
            dq_out[i][...] = (dq.T * scale).astype(dq_out[i].dtype)
        else:
            dq_out[i][...] = dq
    for b in range(blocks):
        acc_out[b][:block, :] = (dk[b] * scale if acc_done else dk[b]).astype(acc_out[b].dtype)
        acc_out[b][block:, :] = dv[b].astype(acc_out[b].dtype)


def total_kernel(parts, levels, place, *refs):
    terms, near_dq, outs = refs[:levels], refs[levels], refs[levels + 1 :]
    total = terms[0][...]
    for term in terms[1:]:
        total = total + term[...].astype(F32)
    rows = total.shape[0] // (2 * parts)
    for m in range(parts):
        outs[m][:rows, :] = total[m * rows : (m + 1) * rows].astype(outs[m].dtype)
        outs[m][rows : 2 * rows, :] = total[(parts + m) * rows : (parts + m + 1) * rows].astype(
            outs[m].dtype
        )
    outs[1][2 * rows :, :] = near_dq[...]


def put_queries(pieces, sources, place, out, stage, sems):
    rows = out.shape[0]
    width = GROUP * HEAD_DIM
    copies = []
    for slot, (m, source) in enumerate(zip(pieces, sources)):
        for i, h in enumerate(HEAD_ORDER):
            first = source.shape[0] - GROUP * rows + i * rows
            stage[slot, :, h * HEAD_DIM : (h + 1) * HEAD_DIM] = source[
                first : first + rows, :
            ].astype(F32)
        col = pl.multiple_of((place[0] ^ m) * width, width)
        copies.append(
            pltpu.make_async_copy(stage.at[slot], out.at[:, pl.ds(col, width)], sems.at[slot])
        )
        copies[-1].start()
    return copies


def first_kernel(pieces, place, *refs):
    out, stage, sems = refs[-3:]
    for copy in put_queries(pieces, refs[: len(pieces)], place, out, stage, sems):
        copy.wait()


def more_kernel(pieces, place, filled, *refs):
    out, stage, sems = refs[-3:]
    for copy in put_queries(pieces, refs[: len(pieces)], place, out, stage, sems):
        copy.wait()


def finish_kernel(parts, place, filled, *refs):
    pieces, refs = refs[:parts], refs[parts:]
    out, out_k, out_v, stage, stage_k, stage_v, sems = refs
    rows = out.shape[0]
    copies = put_queries((1,), (pieces[1],), place, out, stage, sems)
    for m in range(parts):
        col = pl.multiple_of((place[0] ^ m) * HEAD_DIM, HEAD_DIM)
        stage_k[:, pl.ds(col, HEAD_DIM)] = pieces[m][:rows, :].astype(F32)
        stage_v[:, pl.ds(col, HEAD_DIM)] = pieces[m][rows : 2 * rows, :].astype(F32)
    copies.append(pltpu.make_async_copy(stage_k, out_k, sems.at[1]))
    copies.append(pltpu.make_async_copy(stage_v, out_v, sems.at[2]))
    for copy in copies[1:]:
        copy.start()
    for copy in copies:
        copy.wait()


def swap(value, axis, distance):
    return lax.ppermute(value, axis, [(i, i ^ distance) for i in range(lax.axis_size(axis))])


def far_order(levels):
    return [b for b in (2, 3, 1) if b < levels] + list(range(4, levels))


def use_order(levels):
    return [b for b in (2, 1, 3) if b < levels] + list(range(4, levels))


def on_device(queries, key_rows, value_rows, attn_out, out_grad, logsumexp):
    parts = lax.axis_size("head")
    levels = lax.axis_size("ctx").bit_length()
    rows = queries.shape[0]
    block = rows * parts
    span = rows * GROUP
    place = lax.axis_index("head").astype(jnp.int32).reshape(1)

    *rows_in, lse = call(
        functools.partial(load_kernel, parts),
        [vmem(queries.shape, BF16)] * 3
        + [vmem((2 * rows, HEAD_DIM), BF16)] * parts
        + [vmem((8 * parts, 2 * rows), F32)],
        place,
        queries,
        out_grad,
        attn_out,
        key_rows,
        value_rows,
        logsumexp,
        space=pltpu.HBM,
        scratch=[
            vmem(key_rows.shape, BF16),
            vmem(value_rows.shape, BF16),
            vmem(logsumexp.shape, F32),
            pltpu.SemaphoreType.DMA((6,)),
        ],
    )
    kv = rows_in[3:]
    qg = []
    for m in range(parts):
        (packed,) = call(
            functools.partial(pack_kernel, m),
            [vmem((2 * span + DOT_ROWS, HEAD_DIM), BF16)],
            place,
            *rows_in[:3],
        )
        qg.append(packed if m == 0 else swap(packed, "head", m))
    kv = [kv[0]] + [swap(kv[m], "head", m) for m in range(1, parts)]
    (kv_own,) = call(
        functools.partial(join_kernel, parts), [vmem((2 * block, HEAD_DIM), BF16)], place, *kv
    )
    kv_all = [kv_own] + [swap(kv_own, "ctx", 1 << (b - 1)) for b in range(1, levels)]

    dq = [None] * parts
    acc = [None] * levels

    def step(pieces, blocks, dq_done, acc_done):
        has_dq = dq[pieces[0]] is not None
        has_acc = acc[blocks[0]] is not None
        outs = []
        for m in pieces:
            if dq_done:
                outs.append(vmem((span, HEAD_DIM), F32 if m == 0 else BF16))
            else:
                outs.append(vmem((HEAD_DIM, span), F32))
        for b in blocks:
            outs.append(vmem((2 * block, HEAD_DIM), BF16 if acc_done and b > 0 else F32))
        result = call(
            functools.partial(
                step_kernel, pieces, len(blocks), span, has_dq, has_acc, dq_done, acc_done
            ),
            outs,
            place,
            *[qg[m] for m in pieces],
            lse,
            *[kv_all[b] for b in blocks],
            *([dq[m] for m in pieces] if has_dq else []),
            *([acc[b] for b in blocks] if has_acc else []),
        )
        for i, m in enumerate(pieces):
            dq[m] = result[i]
            if dq_done and m > 1:
                dq[m] = swap(dq[m], "head", m)
        for i, b in enumerate(blocks):
            acc[b] = result[len(pieces) + i]
            if acc_done and b > 0:
                acc[b] = swap(acc[b], "ctx", 1 << (b - 1))

    early = tuple(range(parts - 1))
    hops = use_order(levels)
    step((0,), (0,), False, False)
    step((1,), (0,), False, False)
    for b in hops[:-1]:
        step((0, 1), (b,), False, False)
    step(early[2:], (0, *hops[:-1]), False, False)
    step(early, (hops[-1],), True, False)
    for b in far_order(levels) + [0]:
        step((parts - 1,), (b,), b == 0, True)

    dkv = call(
        functools.partial(total_kernel, parts, levels),
        [
            vmem((2 * rows + (span if m == 1 else 0), HEAD_DIM), F32 if m == 0 else BF16)
            for m in range(parts)
        ],
        place,
        *acc,
        dq[1],
    )
    dkv = [dkv[0]] + [swap(dkv[m], "head", m) for m in range(1, parts)]
    width = GROUP * HEAD_DIM

    def stage(count):
        return vmem((count, rows, width), F32)

    (grad_q,) = call(
        functools.partial(first_kernel, (0,)),
        [hbm(queries.shape, F32)],
        place,
        dq[0],
        out_space=pltpu.HBM,
        scratch=[stage(1), pltpu.SemaphoreType.DMA((1,))],
    )
    late = tuple(range(2, parts))
    (grad_q,) = call(
        functools.partial(more_kernel, late),
        [hbm(queries.shape, F32)],
        place,
        *[dq[m] for m in late],
        out_space=pltpu.HBM,
        filled=grad_q,
        scratch=[stage(len(late)), pltpu.SemaphoreType.DMA((len(late),))],
    )
    grad_q, grad_k, grad_v = call(
        functools.partial(finish_kernel, parts),
        [hbm(queries.shape, F32), hbm(key_rows.shape, F32), hbm(value_rows.shape, F32)],
        place,
        *dkv,
        out_space=pltpu.HBM,
        filled=grad_q,
        scratch=[
            stage(1),
            vmem(key_rows.shape, F32),
            vmem(value_rows.shape, F32),
            pltpu.SemaphoreType.DMA((3,)),
        ],
    )
    return (grad_q, grad_k, grad_v)


def solution(mesh):
    rows = P(("ctx", "head"), None)
    return jax.shard_map(
        on_device,
        mesh=mesh,
        in_specs=(rows, rows, rows, rows, rows, P("head", "ctx")),
        out_specs=(rows, rows, rows),
        check_vma=False,
    )
```

```python
import functools
import math

import jax
import jax.numpy as jnp
from jax import lax
from jax.experimental import pallas as pl
from jax.experimental.pallas import tpu as pltpu
from jax.sharding import PartitionSpec as P


HEAD_DIM = 128
GROUP = 8
PAIRS = GROUP // 2
DOT_ROWS = 16
VMEM_BYTES = 16 * 1024 * 1024


F32 = jnp.float32
BF16 = jnp.bfloat16

HEAD_ORDER = [j + half * PAIRS for j in range(PAIRS) for half in range(2)]


def dot_nt(a, b):
    return lax.dot_general(a, b, (((1,), (1,)), ((), ())), preferred_element_type=F32)


def dot_nn(a, b):
    return lax.dot_general(a, b, (((1,), (0,)), ((), ())), preferred_element_type=F32)


def dot_tn(a, b):
    return lax.dot_general(a, b, (((0,), (0,)), ((), ())), preferred_element_type=F32)


def vmem(shape, dtype):
    return pltpu.VMEM(shape, dtype)


def hbm(shape, dtype):
    return jax.ShapeDtypeStruct(shape, dtype)


def call(
    kernel, out_shapes, place, *args, space=pltpu.VMEM, out_space=pltpu.VMEM, filled=None, scratch=()
):
    args = [pltpu.with_memory_space_constraint(a, space) for a in args]
    specs = [pl.BlockSpec(memory_space=pltpu.SMEM)]
    if filled is not None:
        args = [pltpu.with_memory_space_constraint(filled, pltpu.HBM)] + args
        specs += [pl.BlockSpec(memory_space=pltpu.HBM)]
    specs += [pl.BlockSpec(memory_space=space)] * (len(args) + 1 - len(specs))
    return pl.pallas_call(
        kernel,
        out_shape=out_shapes,
        in_specs=specs,
        out_specs=[pl.BlockSpec(memory_space=out_space) for _ in out_shapes],
        scratch_shapes=scratch,
        input_output_aliases={} if filled is None else {1: 0},
        compiler_params=pltpu.CompilerParams(vmem_limit_bytes=VMEM_BYTES),
    )(place, *args)


def load_kernel(parts, place, q_any, g_any, o_any, k_any, v_any, l_any, *refs):
    q_ref, g_ref, o_ref = refs[:3]
    kv_refs, lse_ref = refs[3 : 3 + parts], refs[3 + parts]
    k_ref, v_ref, l_ref, sems = refs[4 + parts :]
    own = place[0]
    rows = k_ref.shape[0]
    pairs = [(k_any, k_ref), (v_any, v_ref), (l_any, l_ref)]
    pairs += [(q_any, q_ref), (g_any, g_ref), (o_any, o_ref)]
    copies = [
        pltpu.make_async_copy(source, target, sems.at[i])
        for i, (source, target) in enumerate(pairs)
    ]
    for copy in copies:
        copy.start()
    for copy in copies[:3]:
        copy.wait()
    for m in range(parts):
        col = pl.multiple_of((own ^ m) * HEAD_DIM, HEAD_DIM)
        kv_refs[m][:rows, :] = k_ref[:, pl.ds(col, HEAD_DIM)]
        kv_refs[m][rows:, :] = v_ref[:, pl.ds(col, HEAD_DIM)]
    for m in range(parts):
        piece = l_ref[:, :rows]
        for c in range(1, parts):
            piece = jnp.where((own ^ m) == c, l_ref[:, c * rows : (c + 1) * rows], piece)
        piece = piece * math.log2(math.e)
        lse_ref[8 * m : 8 * m + PAIRS, :] = jnp.concatenate([piece[:PAIRS], piece[PAIRS:]], axis=1)
        lse_ref[8 * m + PAIRS : 8 * m + 8, :] = jnp.zeros((8 - PAIRS, 2 * rows), F32)
    for copy in copies[3:]:
        copy.wait()


def pack_kernel(m, place, q_ref, g_ref, o_ref, qg_ref):
    rows = q_ref.shape[0]
    span = GROUP * rows
    base = (place[0] ^ m) * (GROUP * HEAD_DIM)
    lane = lax.broadcasted_iota(jnp.int32, (2 * rows, HEAD_DIM), 1)
    dots = jnp.zeros((2 * rows, HEAD_DIM), F32)
    sums = []
    for i, h in enumerate(HEAD_ORDER):
        col = pl.multiple_of(base + h * HEAD_DIM, HEAD_DIM)
        qg_ref[i * rows : (i + 1) * rows, :] = q_ref[:, pl.ds(col, HEAD_DIM)]
        grad = g_ref[:, pl.ds(col, HEAD_DIM)]
        qg_ref[span + i * rows : span + (i + 1) * rows, :] = grad
        prod = grad.astype(F32) * o_ref[:, pl.ds(col, HEAD_DIM)].astype(F32)
        sums.append(jnp.sum(prod, axis=1, keepdims=True))
    for j in range(PAIRS):
        pair = jnp.concatenate([sums[2 * j], sums[2 * j + 1]], axis=0)
        dots = jnp.where(lane == j, pair, dots)
    full = dots.T[:PAIRS, :]
    high = full.astype(BF16).astype(F32)
    mid = (full - high).astype(BF16).astype(F32)
    low = (full - high) - mid
    qg_ref[2 * span :, :] = jnp.concatenate([high, mid, low, jnp.zeros_like(high)], axis=0).astype(
        BF16
    )


def join_kernel(parts, place, *refs):
    pieces, out = refs[:parts], refs[parts]
    rows = out.shape[0] // (2 * parts)
    for m in range(parts):
        out[m * rows : (m + 1) * rows, :] = pieces[m][:rows, :]
        out[(parts + m) * rows : (parts + m + 1) * rows, :] = pieces[m][rows:, :]


def row_of(stack):
    return jnp.concatenate([stack[j : j + 1, :] for j in range(PAIRS)], axis=1)


def step_kernel(pieces, blocks, span, has_dq, has_acc, dq_done, acc_done, place, *refs):
    refs = list(refs)

    def take(count):
        out = refs[:count]
        del refs[:count]
        return out

    qg_refs = take(len(pieces))
    (lse_ref,) = take(1)
    kv_refs = take(blocks)
    dq_in = take(len(pieces)) if has_dq else None
    acc_in = take(blocks) if has_acc else None
    dq_out = take(len(pieces))
    acc_out = take(blocks)
    scale = 1.0 / math.sqrt(HEAD_DIM)
    block = kv_refs[0].shape[0] // 2
    dk = [acc_in[b][:block, :] if has_acc else None for b in range(blocks)]
    dv = [acc_in[b][block:, :] if has_acc else None for b in range(blocks)]
    for i, m in enumerate(pieces):
        query = qg_refs[i][:span, :]
        grad = qg_refs[i][span : 2 * span, :]
        split = qg_refs[i][2 * span : 2 * span + DOT_ROWS, :].astype(F32)
        dots = row_of((split[:PAIRS] + split[PAIRS : 2 * PAIRS]) + split[2 * PAIRS : 3 * PAIRS])
        lse = row_of(lse_ref[8 * m : 8 * m + 8, :])
        dq = dq_in[i][...] if has_dq else None
        for b in range(blocks):
            keys = kv_refs[b][:block, :]
            values = kv_refs[b][block:, :]
            probs = jnp.exp2(dot_nt(keys, query) * (scale * math.log2(math.e)) - lse)
            dprobs = dot_nt(values, grad)
            dscores = (probs * (dprobs - dots)).astype(BF16)
            part_v = dot_nn(probs.astype(BF16), grad)
            part_k = dot_nn(dscores, query)
            part_q = dot_tn(keys, dscores)
            dv[b] = part_v if dv[b] is None else dv[b] + part_v
            dk[b] = part_k if dk[b] is None else dk[b] + part_k
            dq = part_q if dq is None else dq + part_q
        if dq_done:
            dq_out[i][...] = (dq.T * scale).astype(dq_out[i].dtype)
        else:
            dq_out[i][...] = dq
    for b in range(blocks):
        acc_out[b][:block, :] = (dk[b] * scale if acc_done else dk[b]).astype(acc_out[b].dtype)
        acc_out[b][block:, :] = dv[b].astype(acc_out[b].dtype)


def total_kernel(parts, levels, place, *refs):
    terms, outs = refs[:levels], refs[levels:]
    total = terms[0][...]
    for term in terms[1:]:
        total = total + term[...].astype(F32)
    rows = total.shape[0] // (2 * parts)
    for m in range(parts):
        outs[m][:rows, :] = total[m * rows : (m + 1) * rows].astype(outs[m].dtype)
        outs[m][rows : 2 * rows, :] = total[(parts + m) * rows : (parts + m + 1) * rows].astype(
            outs[m].dtype
        )


def put_queries(pieces, sources, place, out, stage, sems):
    rows = out.shape[0]
    width = GROUP * HEAD_DIM
    copies = []
    for slot, (m, source) in enumerate(zip(pieces, sources)):
        for i, h in enumerate(HEAD_ORDER):
            first = source.shape[0] - GROUP * rows + i * rows
            stage[slot, :, h * HEAD_DIM : (h + 1) * HEAD_DIM] = source[
                first : first + rows, :
            ].astype(F32)
        col = pl.multiple_of((place[0] ^ m) * width, width)
        copies.append(
            pltpu.make_async_copy(stage.at[slot], out.at[:, pl.ds(col, width)], sems.at[slot])
        )
        copies[-1].start()
    return copies


def first_kernel(pieces, place, *refs):
    out, stage, sems = refs[-3:]
    for copy in put_queries(pieces, refs[: len(pieces)], place, out, stage, sems):
        copy.wait()


def more_kernel(pieces, place, filled, *refs):
    out, stage, sems = refs[-3:]
    for copy in put_queries(pieces, refs[: len(pieces)], place, out, stage, sems):
        copy.wait()


def finish_kernel(parts, place, *refs):
    pieces, (out_k, out_v, stage_k, stage_v, sems) = refs[:parts], refs[parts:]
    for m in range(parts):
        rows = out_k.shape[0]
        col = pl.multiple_of((place[0] ^ m) * HEAD_DIM, HEAD_DIM)
        stage_k[:, pl.ds(col, HEAD_DIM)] = pieces[m][:rows, :].astype(F32)
        stage_v[:, pl.ds(col, HEAD_DIM)] = pieces[m][rows:, :].astype(F32)
    copies = [
        pltpu.make_async_copy(stage_k, out_k, sems.at[0]),
        pltpu.make_async_copy(stage_v, out_v, sems.at[1]),
    ]
    for copy in copies:
        copy.start()
    for copy in copies:
        copy.wait()


def swap(value, axis, distance):
    return lax.ppermute(value, axis, [(i, i ^ distance) for i in range(lax.axis_size(axis))])


def far_order(levels):
    return [b for b in (2, 3, 1) if b < levels] + list(range(4, levels))


def use_order(levels):
    return [b for b in (1, 2, 3) if b < levels] + list(range(4, levels))


def on_device(queries, key_rows, value_rows, attn_out, out_grad, logsumexp):
    parts = lax.axis_size("head")
    levels = lax.axis_size("ctx").bit_length()
    rows = queries.shape[0]
    block = rows * parts
    span = rows * GROUP
    place = lax.axis_index("head").astype(jnp.int32).reshape(1)

    *rows_in, lse = call(
        functools.partial(load_kernel, parts),
        [vmem(queries.shape, BF16)] * 3
        + [vmem((2 * rows, HEAD_DIM), BF16)] * parts
        + [vmem((8 * parts, 2 * rows), F32)],
        place,
        queries,
        out_grad,
        attn_out,
        key_rows,
        value_rows,
        logsumexp,
        space=pltpu.HBM,
        scratch=[
            vmem(key_rows.shape, BF16),
            vmem(value_rows.shape, BF16),
            vmem(logsumexp.shape, F32),
            pltpu.SemaphoreType.DMA((6,)),
        ],
    )
    kv = rows_in[3:]
    qg = []
    for m in range(parts):
        (packed,) = call(
            functools.partial(pack_kernel, m),
            [vmem((2 * span + DOT_ROWS, HEAD_DIM), BF16)],
            place,
            *rows_in[:3],
        )
        qg.append(packed if m == 0 else swap(packed, "head", m))
    kv = [kv[0]] + [swap(kv[m], "head", m) for m in range(1, parts)]
    (kv_own,) = call(
        functools.partial(join_kernel, parts), [vmem((2 * block, HEAD_DIM), BF16)], place, *kv
    )
    kv_all = [kv_own] + [swap(kv_own, "ctx", 1 << (b - 1)) for b in range(1, levels)]

    dq = [None] * parts
    acc = [None] * levels

    def step(pieces, blocks, dq_done, acc_done):
        has_dq = dq[pieces[0]] is not None
        has_acc = acc[blocks[0]] is not None
        outs = []
        for m in pieces:
            if dq_done:
                outs.append(vmem((span, HEAD_DIM), F32 if m == 0 else BF16))
            else:
                outs.append(vmem((HEAD_DIM, span), F32))
        for b in blocks:
            outs.append(vmem((2 * block, HEAD_DIM), BF16 if acc_done and b > 0 else F32))
        result = call(
            functools.partial(
                step_kernel, pieces, len(blocks), span, has_dq, has_acc, dq_done, acc_done
            ),
            outs,
            place,
            *[qg[m] for m in pieces],
            lse,
            *[kv_all[b] for b in blocks],
            *([dq[m] for m in pieces] if has_dq else []),
            *([acc[b] for b in blocks] if has_acc else []),
        )
        for i, m in enumerate(pieces):
            dq[m] = result[i]
            if dq_done and m > 0:
                dq[m] = swap(dq[m], "head", m)
        for i, b in enumerate(blocks):
            acc[b] = result[len(pieces) + i]
            if acc_done and b > 0:
                acc[b] = swap(acc[b], "ctx", 1 << (b - 1))

    early = tuple(range(parts - 1))
    hops = use_order(levels)
    step((0,), (0,), False, False)
    step((1,), (0,), False, False)
    for b in hops[:-1]:
        step((0, 1), (b,), False, False)
    step(early[2:], (0, *hops[:-1]), False, False)
    step(early, (hops[-1],), True, False)
    for b in far_order(levels) + [0]:
        step((parts - 1,), (b,), b == 0, True)

    dkv = call(
        functools.partial(total_kernel, parts, levels),
        [
            vmem((2 * rows, HEAD_DIM), F32 if m == 0 else BF16) for m in range(parts)
        ],
        place,
        *acc,
    )
    dkv = [dkv[0]] + [swap(dkv[m], "head", m) for m in range(1, parts)]
    width = GROUP * HEAD_DIM

    def stage(count):
        return vmem((count, rows, width), F32)

    (grad_q,) = call(
        functools.partial(first_kernel, (0,)),
        [hbm(queries.shape, F32)],
        place,
        dq[0],
        out_space=pltpu.HBM,
        scratch=[stage(1), pltpu.SemaphoreType.DMA((1,))],
    )
    late = tuple(range(1, parts))
    (grad_q,) = call(
        functools.partial(more_kernel, late),
        [hbm(queries.shape, F32)],
        place,
        *[dq[m] for m in late],
        out_space=pltpu.HBM,
        filled=grad_q,
        scratch=[stage(len(late)), pltpu.SemaphoreType.DMA((len(late),))],
    )
    grad_k, grad_v = call(
        functools.partial(finish_kernel, parts),
        [hbm(key_rows.shape, F32), hbm(value_rows.shape, F32)],
        place,
        *dkv,
        out_space=pltpu.HBM,
        scratch=[
            vmem(key_rows.shape, F32),
            vmem(value_rows.shape, F32),
            pltpu.SemaphoreType.DMA((2,)),
        ],
    )
    return (grad_q, grad_k, grad_v)


def solution(mesh):
    rows = P(("ctx", "head"), None)
    return jax.shard_map(
        on_device,
        mesh=mesh,
        in_specs=(rows, rows, rows, rows, rows, P("head", "ctx")),
        out_specs=(rows, rows, rows),
        check_vma=False,
    )
```

```python
import functools
import math

import jax
import jax.numpy as jnp
from jax import lax
from jax.experimental import pallas as pl
from jax.experimental.pallas import tpu as pltpu
from jax.sharding import PartitionSpec as P


HEAD_DIM = 128
GROUP = 8
PAIRS = GROUP // 2
DOT_ROWS = 16
VMEM_BYTES = 16 * 1024 * 1024


F32 = jnp.float32
BF16 = jnp.bfloat16

HEAD_ORDER = [j + half * PAIRS for j in range(PAIRS) for half in range(2)]


def dot_nt(a, b):
    return lax.dot_general(a, b, (((1,), (1,)), ((), ())), preferred_element_type=F32)


def dot_nn(a, b):
    return lax.dot_general(a, b, (((1,), (0,)), ((), ())), preferred_element_type=F32)


def dot_tn(a, b):
    return lax.dot_general(a, b, (((0,), (0,)), ((), ())), preferred_element_type=F32)


def vmem(shape, dtype):
    return pltpu.VMEM(shape, dtype)


def hbm(shape, dtype):
    return jax.ShapeDtypeStruct(shape, dtype)


def call(
    kernel, out_shapes, place, *args, space=pltpu.VMEM, out_space=pltpu.VMEM, filled=None, scratch=()
):
    args = [pltpu.with_memory_space_constraint(a, space) for a in args]
    specs = [pl.BlockSpec(memory_space=pltpu.SMEM)]
    if filled is not None:
        args = [pltpu.with_memory_space_constraint(filled, pltpu.HBM)] + args
        specs += [pl.BlockSpec(memory_space=pltpu.HBM)]
    specs += [pl.BlockSpec(memory_space=space)] * (len(args) + 1 - len(specs))
    return pl.pallas_call(
        kernel,
        out_shape=out_shapes,
        in_specs=specs,
        out_specs=[pl.BlockSpec(memory_space=out_space) for _ in out_shapes],
        scratch_shapes=scratch,
        input_output_aliases={} if filled is None else {1: 0},
        compiler_params=pltpu.CompilerParams(vmem_limit_bytes=VMEM_BYTES),
    )(place, *args)


def load_kernel(parts, place, q_any, g_any, o_any, k_any, v_any, l_any, *refs):
    q_ref, g_ref, o_ref = refs[:3]
    kv_refs, lse_ref = refs[3 : 3 + parts], refs[3 + parts]
    k_ref, v_ref, l_ref, sems = refs[4 + parts :]
    own = place[0]
    rows = k_ref.shape[0]
    pairs = [(k_any, k_ref), (v_any, v_ref), (l_any, l_ref)]
    pairs += [(q_any, q_ref), (g_any, g_ref), (o_any, o_ref)]
    copies = [
        pltpu.make_async_copy(source, target, sems.at[i])
        for i, (source, target) in enumerate(pairs)
    ]
    for copy in copies:
        copy.start()
    for copy in copies[:3]:
        copy.wait()
    for m in range(parts):
        col = pl.multiple_of((own ^ m) * HEAD_DIM, HEAD_DIM)
        kv_refs[m][:rows, :] = k_ref[:, pl.ds(col, HEAD_DIM)]
        kv_refs[m][rows:, :] = v_ref[:, pl.ds(col, HEAD_DIM)]
    for m in range(parts):
        piece = l_ref[:, :rows]
        for c in range(1, parts):
            piece = jnp.where((own ^ m) == c, l_ref[:, c * rows : (c + 1) * rows], piece)
        piece = piece * math.log2(math.e)
        lse_ref[8 * m : 8 * m + PAIRS, :] = jnp.concatenate([piece[:PAIRS], piece[PAIRS:]], axis=1)
        lse_ref[8 * m + PAIRS : 8 * m + 8, :] = jnp.zeros((8 - PAIRS, 2 * rows), F32)
    for copy in copies[3:]:
        copy.wait()


def pack_kernel(m, place, q_ref, g_ref, o_ref, qg_ref):
    rows = q_ref.shape[0]
    span = GROUP * rows
    base = (place[0] ^ m) * (GROUP * HEAD_DIM)
    lane = lax.broadcasted_iota(jnp.int32, (2 * rows, HEAD_DIM), 1)
    dots = jnp.zeros((2 * rows, HEAD_DIM), F32)
    sums = []
    for i, h in enumerate(HEAD_ORDER):
        col = pl.multiple_of(base + h * HEAD_DIM, HEAD_DIM)
        qg_ref[i * rows : (i + 1) * rows, :] = q_ref[:, pl.ds(col, HEAD_DIM)]
        grad = g_ref[:, pl.ds(col, HEAD_DIM)]
        qg_ref[span + i * rows : span + (i + 1) * rows, :] = grad
        prod = grad.astype(F32) * o_ref[:, pl.ds(col, HEAD_DIM)].astype(F32)
        sums.append(jnp.sum(prod, axis=1, keepdims=True))
    for j in range(PAIRS):
        pair = jnp.concatenate([sums[2 * j], sums[2 * j + 1]], axis=0)
        dots = jnp.where(lane == j, pair, dots)
    full = dots.T[:PAIRS, :]
    high = full.astype(BF16).astype(F32)
    mid = (full - high).astype(BF16).astype(F32)
    low = (full - high) - mid
    qg_ref[2 * span :, :] = jnp.concatenate([high, mid, low, jnp.zeros_like(high)], axis=0).astype(
        BF16
    )


def join_kernel(parts, place, *refs):
    pieces, out = refs[:parts], refs[parts]
    rows = out.shape[0] // (2 * parts)
    for m in range(parts):
        out[m * rows : (m + 1) * rows, :] = pieces[m][:rows, :]
        out[(parts + m) * rows : (parts + m + 1) * rows, :] = pieces[m][rows:, :]


def row_of(stack):
    return jnp.concatenate([stack[j : j + 1, :] for j in range(PAIRS)], axis=1)


def step_kernel(pieces, blocks, span, has_dq, has_acc, dq_done, acc_done, place, *refs):
    refs = list(refs)

    def take(count):
        out = refs[:count]
        del refs[:count]
        return out

    qg_refs = take(len(pieces))
    (lse_ref,) = take(1)
    kv_refs = take(blocks)
    dq_in = take(len(pieces)) if has_dq else None
    acc_in = take(blocks) if has_acc else None
    dq_out = take(len(pieces))
    acc_out = take(blocks)
    scale = 1.0 / math.sqrt(HEAD_DIM)
    block = kv_refs[0].shape[0] // 2
    dk = [acc_in[b][:block, :] if has_acc else None for b in range(blocks)]
    dv = [acc_in[b][block:, :] if has_acc else None for b in range(blocks)]
    for i, m in enumerate(pieces):
        query = qg_refs[i][:span, :]
        grad = qg_refs[i][span : 2 * span, :]
        split = qg_refs[i][2 * span : 2 * span + DOT_ROWS, :].astype(F32)
        dots = row_of((split[:PAIRS] + split[PAIRS : 2 * PAIRS]) + split[2 * PAIRS : 3 * PAIRS])
        lse = row_of(lse_ref[8 * m : 8 * m + 8, :])
        dq = dq_in[i][...] if has_dq else None
        for b in range(blocks):
            keys = kv_refs[b][:block, :]
            values = kv_refs[b][block:, :]
            probs = jnp.exp2(dot_nt(keys, query) * (scale * math.log2(math.e)) - lse)
            dprobs = dot_nt(values, grad)
            dscores = (probs * (dprobs - dots)).astype(BF16)
            part_v = dot_nn(probs.astype(BF16), grad)
            part_k = dot_nn(dscores, query)
            part_q = dot_tn(keys, dscores)
            dv[b] = part_v if dv[b] is None else dv[b] + part_v
            dk[b] = part_k if dk[b] is None else dk[b] + part_k
            dq = part_q if dq is None else dq + part_q
        if dq_done:
            dq_out[i][...] = (dq.T * scale).astype(dq_out[i].dtype)
        else:
            dq_out[i][...] = dq
    for b in range(blocks):
        acc_out[b][:block, :] = (dk[b] * scale if acc_done else dk[b]).astype(acc_out[b].dtype)
        acc_out[b][block:, :] = dv[b].astype(acc_out[b].dtype)


def total_kernel(parts, levels, place, *refs):
    terms, outs = refs[:levels], refs[levels:]
    total = terms[0][...]
    for term in terms[1:]:
        total = total + term[...].astype(F32)
    rows = total.shape[0] // (2 * parts)
    for m in range(parts):
        outs[m][:rows, :] = total[m * rows : (m + 1) * rows].astype(outs[m].dtype)
        outs[m][rows : 2 * rows, :] = total[(parts + m) * rows : (parts + m + 1) * rows].astype(
            outs[m].dtype
        )


def put_queries(pieces, sources, place, out, stage, sems):
    rows = out.shape[0]
    width = GROUP * HEAD_DIM
    copies = []
    for slot, (m, source) in enumerate(zip(pieces, sources)):
        for i, h in enumerate(HEAD_ORDER):
            first = source.shape[0] - GROUP * rows + i * rows
            stage[slot, :, h * HEAD_DIM : (h + 1) * HEAD_DIM] = source[
                first : first + rows, :
            ].astype(F32)
        col = pl.multiple_of((place[0] ^ m) * width, width)
        copies.append(
            pltpu.make_async_copy(stage.at[slot], out.at[:, pl.ds(col, width)], sems.at[slot])
        )
        copies[-1].start()
    return copies


def first_kernel(pieces, place, *refs):
    out, stage, sems = refs[-3:]
    for copy in put_queries(pieces, refs[: len(pieces)], place, out, stage, sems):
        copy.wait()


def more_kernel(pieces, place, filled, *refs):
    out, stage, sems = refs[-3:]
    for copy in put_queries(pieces, refs[: len(pieces)], place, out, stage, sems):
        copy.wait()


def finish_kernel(parts, place, *refs):
    pieces, (out_k, out_v, stage_k, stage_v, sems) = refs[:parts], refs[parts:]
    for m in range(parts):
        rows = out_k.shape[0]
        col = pl.multiple_of((place[0] ^ m) * HEAD_DIM, HEAD_DIM)
        stage_k[:, pl.ds(col, HEAD_DIM)] = pieces[m][:rows, :].astype(F32)
        stage_v[:, pl.ds(col, HEAD_DIM)] = pieces[m][rows:, :].astype(F32)
    copies = [
        pltpu.make_async_copy(stage_k, out_k, sems.at[0]),
        pltpu.make_async_copy(stage_v, out_v, sems.at[1]),
    ]
    for copy in copies:
        copy.start()
    for copy in copies:
        copy.wait()


def partner_bit(slot, core, levels):
    maps = ((0, 1, 2), (1, 2, 0))
    return maps[core][slot - 1] if slot <= 3 and levels >= 4 else slot - 1


def trade(value, slot, levels):
    ctx, head = lax.axis_size("ctx"), lax.axis_size("head")
    pairs = [
        (i * head + h, (i ^ 1 << partner_bit(slot, h % 2, levels)) * head + h)
        for i in range(ctx)
        for h in range(head)
    ]
    return lax.ppermute(value, ("ctx", "head"), pairs)


def swap(value, axis, distance):
    return lax.ppermute(value, axis, [(i, i ^ distance) for i in range(lax.axis_size(axis))])


def far_order(levels):
    return [b for b in (1, 2, 3) if b < levels] + list(range(4, levels))


def use_order(levels):
    return [b for b in (1, 2, 3) if b < levels] + list(range(4, levels))


def on_device(queries, key_rows, value_rows, attn_out, out_grad, logsumexp):
    parts = lax.axis_size("head")
    levels = lax.axis_size("ctx").bit_length()
    rows = queries.shape[0]
    block = rows * parts
    span = rows * GROUP
    place = lax.axis_index("head").astype(jnp.int32).reshape(1)

    *rows_in, lse = call(
        functools.partial(load_kernel, parts),
        [vmem(queries.shape, BF16)] * 3
        + [vmem((2 * rows, HEAD_DIM), BF16)] * parts
        + [vmem((8 * parts, 2 * rows), F32)],
        place,
        queries,
        out_grad,
        attn_out,
        key_rows,
        value_rows,
        logsumexp,
        space=pltpu.HBM,
        scratch=[
            vmem(key_rows.shape, BF16),
            vmem(value_rows.shape, BF16),
            vmem(logsumexp.shape, F32),
            pltpu.SemaphoreType.DMA((6,)),
        ],
    )
    kv = rows_in[3:]
    qg = []
    for m in range(parts):
        (packed,) = call(
            functools.partial(pack_kernel, m),
            [vmem((2 * span + DOT_ROWS, HEAD_DIM), BF16)],
            place,
            *rows_in[:3],
        )
        qg.append(packed if m == 0 else swap(packed, "head", m))
    kv = [kv[0]] + [swap(kv[m], "head", m) for m in range(1, parts)]
    (kv_own,) = call(
        functools.partial(join_kernel, parts), [vmem((2 * block, HEAD_DIM), BF16)], place, *kv
    )
    kv_all = [kv_own] + [trade(kv_own, b, levels) for b in range(1, levels)]

    dq = [None] * parts
    acc = [None] * levels

    def step(pieces, blocks, dq_done, acc_done):
        has_dq = dq[pieces[0]] is not None
        has_acc = acc[blocks[0]] is not None
        outs = []
        for m in pieces:
            if dq_done:
                outs.append(vmem((span, HEAD_DIM), F32 if m == 0 else BF16))
            else:
                outs.append(vmem((HEAD_DIM, span), F32))
        for b in blocks:
            outs.append(vmem((2 * block, HEAD_DIM), BF16 if acc_done and b > 0 else F32))
        result = call(
            functools.partial(
                step_kernel, pieces, len(blocks), span, has_dq, has_acc, dq_done, acc_done
            ),
            outs,
            place,
            *[qg[m] for m in pieces],
            lse,
            *[kv_all[b] for b in blocks],
            *([dq[m] for m in pieces] if has_dq else []),
            *([acc[b] for b in blocks] if has_acc else []),
        )
        for i, m in enumerate(pieces):
            dq[m] = result[i]
            if dq_done and m > 0:
                dq[m] = swap(dq[m], "head", m)
        for i, b in enumerate(blocks):
            acc[b] = result[len(pieces) + i]
            if acc_done and b > 0:
                acc[b] = trade(acc[b], b, levels)

    early = tuple(range(parts - 1))
    hops = use_order(levels)
    step((0,), (0,), False, False)
    step((1,), (0,), False, False)
    for b in hops[:-1]:
        step((0, 1), (b,), False, False)
    step(early[2:], (0, *hops[:-1]), False, False)
    step(early, (hops[-1],), True, False)
    for b in far_order(levels) + [0]:
        step((parts - 1,), (b,), b == 0, True)

    dkv = call(
        functools.partial(total_kernel, parts, levels),
        [
            vmem((2 * rows, HEAD_DIM), F32 if m == 0 else BF16) for m in range(parts)
        ],
        place,
        *acc,
    )
    dkv = [dkv[0]] + [swap(dkv[m], "head", m) for m in range(1, parts)]
    width = GROUP * HEAD_DIM

    def stage(count):
        return vmem((count, rows, width), F32)

    (grad_q,) = call(
        functools.partial(first_kernel, (0,)),
        [hbm(queries.shape, F32)],
        place,
        dq[0],
        out_space=pltpu.HBM,
        scratch=[stage(1), pltpu.SemaphoreType.DMA((1,))],
    )
    late = tuple(range(1, parts))
    (grad_q,) = call(
        functools.partial(more_kernel, late),
        [hbm(queries.shape, F32)],
        place,
        *[dq[m] for m in late],
        out_space=pltpu.HBM,
        filled=grad_q,
        scratch=[stage(len(late)), pltpu.SemaphoreType.DMA((len(late),))],
    )
    grad_k, grad_v = call(
        functools.partial(finish_kernel, parts),
        [hbm(key_rows.shape, F32), hbm(value_rows.shape, F32)],
        place,
        *dkv,
        out_space=pltpu.HBM,
        scratch=[
            vmem(key_rows.shape, F32),
            vmem(value_rows.shape, F32),
            pltpu.SemaphoreType.DMA((2,)),
        ],
    )
    return (grad_q, grad_k, grad_v)


def solution(mesh):
    rows = P(("ctx", "head"), None)
    return jax.shard_map(
        on_device,
        mesh=mesh,
        in_specs=(rows, rows, rows, rows, rows, P("head", "ctx")),
        out_specs=(rows, rows, rows),
        check_vma=False,
    )
```

```python
import functools
import math

import jax
import jax.numpy as jnp
from jax import lax
from jax.experimental import pallas as pl
from jax.experimental.pallas import tpu as pltpu
from jax.sharding import PartitionSpec as P


HEAD_DIM = 128
GROUP = 8
PAIRS = GROUP // 2
DOT_ROWS = 16
VMEM_BYTES = 16 * 1024 * 1024


F32 = jnp.float32
BF16 = jnp.bfloat16

HEAD_ORDER = [j + half * PAIRS for j in range(PAIRS) for half in range(2)]


def dot_nt(a, b):
    return lax.dot_general(a, b, (((1,), (1,)), ((), ())), preferred_element_type=F32)


def dot_nn(a, b):
    return lax.dot_general(a, b, (((1,), (0,)), ((), ())), preferred_element_type=F32)


def vmem(shape, dtype):
    return pltpu.VMEM(shape, dtype)


def hbm(shape, dtype):
    return jax.ShapeDtypeStruct(shape, dtype)


def call(
    kernel, out_shapes, place, *args, space=pltpu.VMEM, out_space=pltpu.VMEM, filled=None, scratch=()
):
    args = [pltpu.with_memory_space_constraint(a, space) for a in args]
    specs = [pl.BlockSpec(memory_space=pltpu.SMEM)]
    if filled is not None:
        args = [pltpu.with_memory_space_constraint(filled, pltpu.HBM)] + args
        specs += [pl.BlockSpec(memory_space=pltpu.HBM)]
    specs += [pl.BlockSpec(memory_space=space)] * (len(args) + 1 - len(specs))
    return pl.pallas_call(
        kernel,
        out_shape=out_shapes,
        in_specs=specs,
        out_specs=[pl.BlockSpec(memory_space=out_space) for _ in out_shapes],
        scratch_shapes=scratch,
        input_output_aliases={} if filled is None else {1: 0},
        compiler_params=pltpu.CompilerParams(vmem_limit_bytes=VMEM_BYTES),
    )(place, *args)


def load_kernel(parts, place, q_any, g_any, o_any, k_any, v_any, l_any, *refs):
    q_ref, g_ref, o_ref = refs[:3]
    kv_refs, lse_ref = refs[3 : 3 + parts], refs[3 + parts]
    k_ref, v_ref, l_ref, sems = refs[4 + parts :]
    own = place[0]
    rows = k_ref.shape[0]
    pairs = [(k_any, k_ref), (v_any, v_ref), (l_any, l_ref)]
    pairs += [(q_any, q_ref), (g_any, g_ref), (o_any, o_ref)]
    copies = [
        pltpu.make_async_copy(source, target, sems.at[i])
        for i, (source, target) in enumerate(pairs)
    ]
    for copy in copies:
        copy.start()
    for copy in copies[:3]:
        copy.wait()
    for m in range(parts):
        col = pl.multiple_of((own ^ m) * HEAD_DIM, HEAD_DIM)
        kv_refs[m][:rows, :] = k_ref[:, pl.ds(col, HEAD_DIM)]
        kv_refs[m][rows:, :] = v_ref[:, pl.ds(col, HEAD_DIM)]
    for m in range(parts):
        piece = l_ref[:, :rows]
        for c in range(1, parts):
            piece = jnp.where((own ^ m) == c, l_ref[:, c * rows : (c + 1) * rows], piece)
        piece = piece * math.log2(math.e)
        lse_ref[8 * m : 8 * m + PAIRS, :] = jnp.concatenate([piece[:PAIRS], piece[PAIRS:]], axis=1)
        lse_ref[8 * m + PAIRS : 8 * m + 8, :] = jnp.zeros((8 - PAIRS, 2 * rows), F32)
    for copy in copies[3:]:
        copy.wait()


def pack_kernel(m, place, q_ref, g_ref, o_ref, qg_ref):
    rows = q_ref.shape[0]
    span = GROUP * rows
    base = (place[0] ^ m) * (GROUP * HEAD_DIM)
    lane = lax.broadcasted_iota(jnp.int32, (2 * rows, HEAD_DIM), 1)
    dots = jnp.zeros((2 * rows, HEAD_DIM), F32)
    sums = []
    for i, h in enumerate(HEAD_ORDER):
        col = pl.multiple_of(base + h * HEAD_DIM, HEAD_DIM)
        qg_ref[i * rows : (i + 1) * rows, :] = q_ref[:, pl.ds(col, HEAD_DIM)]
        grad = g_ref[:, pl.ds(col, HEAD_DIM)]
        qg_ref[span + i * rows : span + (i + 1) * rows, :] = grad
        prod = grad.astype(F32) * o_ref[:, pl.ds(col, HEAD_DIM)].astype(F32)
        sums.append(jnp.sum(prod, axis=1, keepdims=True))
    for j in range(PAIRS):
        pair = jnp.concatenate([sums[2 * j], sums[2 * j + 1]], axis=0)
        dots = jnp.where(lane == j, pair, dots)
    full = dots.T[:PAIRS, :]
    high = full.astype(BF16).astype(F32)
    mid = (full - high).astype(BF16).astype(F32)
    low = (full - high) - mid
    qg_ref[2 * span :, :] = jnp.concatenate([high, mid, low, jnp.zeros_like(high)], axis=0).astype(
        BF16
    )


def join_kernel(parts, place, *refs):
    pieces, out = refs[:parts], refs[parts]
    rows = out.shape[0] // (2 * parts)
    for m in range(parts):
        out[m * rows : (m + 1) * rows, :] = pieces[m][:rows, :]
        out[(parts + m) * rows : (parts + m + 1) * rows, :] = pieces[m][rows:, :]


def row_of(stack):
    return jnp.concatenate([stack[j : j + 1, :] for j in range(PAIRS)], axis=1)


def step_kernel(pieces, blocks, span, has_dq, has_acc, dq_done, acc_done, place, *refs):
    refs = list(refs)

    def take(count):
        out = refs[:count]
        del refs[:count]
        return out

    qg_refs = take(len(pieces))
    (lse_ref,) = take(1)
    kv_refs = take(blocks)
    dq_in = take(len(pieces)) if has_dq else None
    acc_in = take(blocks) if has_acc else None
    dq_out = take(len(pieces))
    acc_out = take(blocks)
    scale = 1.0 / math.sqrt(HEAD_DIM)
    block = kv_refs[0].shape[0] // 2
    dk = [acc_in[b][:block, :] if has_acc else None for b in range(blocks)]
    dv = [acc_in[b][block:, :] if has_acc else None for b in range(blocks)]
    turned = [kv_refs[b][:block, :].T for b in range(blocks)]
    for i, m in enumerate(pieces):
        query = qg_refs[i][:span, :]
        grad = qg_refs[i][span : 2 * span, :]
        split = qg_refs[i][2 * span : 2 * span + DOT_ROWS, :].astype(F32)
        dots = row_of((split[:PAIRS] + split[PAIRS : 2 * PAIRS]) + split[2 * PAIRS : 3 * PAIRS])
        lse = row_of(lse_ref[8 * m : 8 * m + 8, :])
        dq = dq_in[i][...] if has_dq else None
        for b in range(blocks):
            keys = kv_refs[b][:block, :]
            values = kv_refs[b][block:, :]
            probs = jnp.exp2(dot_nt(keys, query) * (scale * math.log2(math.e)) - lse)
            dprobs = dot_nt(values, grad)
            dscores = (probs * (dprobs - dots)).astype(BF16)
            part_v = dot_nn(probs.astype(BF16), grad)
            part_k = dot_nn(dscores, query)
            part_q = dot_nn(turned[b], dscores)
            dv[b] = part_v if dv[b] is None else dv[b] + part_v
            dk[b] = part_k if dk[b] is None else dk[b] + part_k
            dq = part_q if dq is None else dq + part_q
        if dq_done:
            dq_out[i][...] = (dq.T * scale).astype(dq_out[i].dtype)
        else:
            dq_out[i][...] = dq
    for b in range(blocks):
        acc_out[b][:block, :] = (dk[b] * scale if acc_done else dk[b]).astype(acc_out[b].dtype)
        acc_out[b][block:, :] = dv[b].astype(acc_out[b].dtype)


def total_kernel(parts, levels, place, *refs):
    terms, outs = refs[:levels], refs[levels:]
    total = terms[0][...]
    for term in terms[1:]:
        total = total + term[...].astype(F32)
    rows = total.shape[0] // (2 * parts)
    for m in range(parts):
        outs[m][:rows, :] = total[m * rows : (m + 1) * rows].astype(outs[m].dtype)
        outs[m][rows : 2 * rows, :] = total[(parts + m) * rows : (parts + m + 1) * rows].astype(
            outs[m].dtype
        )


def put_queries(pieces, sources, place, out, stage, sems):
    rows = out.shape[0]
    width = GROUP * HEAD_DIM
    copies = []
    for slot, (m, source) in enumerate(zip(pieces, sources)):
        for i, h in enumerate(HEAD_ORDER):
            first = source.shape[0] - GROUP * rows + i * rows
            stage[slot, :, h * HEAD_DIM : (h + 1) * HEAD_DIM] = source[
                first : first + rows, :
            ].astype(F32)
        col = pl.multiple_of((place[0] ^ m) * width, width)
        copies.append(
            pltpu.make_async_copy(stage.at[slot], out.at[:, pl.ds(col, width)], sems.at[slot])
        )
        copies[-1].start()
    return copies


def first_kernel(pieces, place, *refs):
    out, stage, sems = refs[-3:]
    for copy in put_queries(pieces, refs[: len(pieces)], place, out, stage, sems):
        copy.wait()


def more_kernel(pieces, place, filled, *refs):
    out, stage, sems = refs[-3:]
    for copy in put_queries(pieces, refs[: len(pieces)], place, out, stage, sems):
        copy.wait()


def finish_kernel(parts, place, *refs):
    pieces, (out_k, out_v, stage_k, stage_v, sems) = refs[:parts], refs[parts:]
    for m in range(parts):
        rows = out_k.shape[0]
        col = pl.multiple_of((place[0] ^ m) * HEAD_DIM, HEAD_DIM)
        stage_k[:, pl.ds(col, HEAD_DIM)] = pieces[m][:rows, :].astype(F32)
        stage_v[:, pl.ds(col, HEAD_DIM)] = pieces[m][rows:, :].astype(F32)
    copies = [
        pltpu.make_async_copy(stage_k, out_k, sems.at[0]),
        pltpu.make_async_copy(stage_v, out_v, sems.at[1]),
    ]
    for copy in copies:
        copy.start()
    for copy in copies:
        copy.wait()


def partner_bit(slot, core, levels):
    maps = ((0, 1, 2), (1, 2, 0))
    return maps[core][slot - 1] if slot <= 3 and levels >= 4 else slot - 1


def trade(value, slot, levels):
    ctx, head = lax.axis_size("ctx"), lax.axis_size("head")
    pairs = [
        (i * head + h, (i ^ 1 << partner_bit(slot, h % 2, levels)) * head + h)
        for i in range(ctx)
        for h in range(head)
    ]
    return lax.ppermute(value, ("ctx", "head"), pairs)


def swap(value, axis, distance):
    return lax.ppermute(value, axis, [(i, i ^ distance) for i in range(lax.axis_size(axis))])


def far_order(levels):
    return [b for b in (1, 2, 3) if b < levels] + list(range(4, levels))


def use_order(levels):
    return [b for b in (1, 2, 3) if b < levels] + list(range(4, levels))


def on_device(queries, key_rows, value_rows, attn_out, out_grad, logsumexp):
    parts = lax.axis_size("head")
    levels = lax.axis_size("ctx").bit_length()
    rows = queries.shape[0]
    block = rows * parts
    span = rows * GROUP
    place = lax.axis_index("head").astype(jnp.int32).reshape(1)

    *rows_in, lse = call(
        functools.partial(load_kernel, parts),
        [vmem(queries.shape, BF16)] * 3
        + [vmem((2 * rows, HEAD_DIM), BF16)] * parts
        + [vmem((8 * parts, 2 * rows), F32)],
        place,
        queries,
        out_grad,
        attn_out,
        key_rows,
        value_rows,
        logsumexp,
        space=pltpu.HBM,
        scratch=[
            vmem(key_rows.shape, BF16),
            vmem(value_rows.shape, BF16),
            vmem(logsumexp.shape, F32),
            pltpu.SemaphoreType.DMA((6,)),
        ],
    )
    kv = rows_in[3:]
    qg = []
    for m in range(parts):
        (packed,) = call(
            functools.partial(pack_kernel, m),
            [vmem((2 * span + DOT_ROWS, HEAD_DIM), BF16)],
            place,
            *rows_in[:3],
        )
        qg.append(packed if m == 0 else swap(packed, "head", m))
    kv = [kv[0]] + [swap(kv[m], "head", m) for m in range(1, parts)]
    (kv_own,) = call(
        functools.partial(join_kernel, parts), [vmem((2 * block, HEAD_DIM), BF16)], place, *kv
    )
    kv_all = [kv_own] + [trade(kv_own, b, levels) for b in range(1, levels)]

    dq = [None] * parts
    acc = [None] * levels

    def step(pieces, blocks, dq_done, acc_done):
        has_dq = dq[pieces[0]] is not None
        has_acc = acc[blocks[0]] is not None
        outs = []
        for m in pieces:
            if dq_done:
                outs.append(vmem((span, HEAD_DIM), F32 if m == 0 else BF16))
            else:
                outs.append(vmem((HEAD_DIM, span), F32))
        for b in blocks:
            outs.append(vmem((2 * block, HEAD_DIM), BF16 if acc_done and b > 0 else F32))
        result = call(
            functools.partial(
                step_kernel, pieces, len(blocks), span, has_dq, has_acc, dq_done, acc_done
            ),
            outs,
            place,
            *[qg[m] for m in pieces],
            lse,
            *[kv_all[b] for b in blocks],
            *([dq[m] for m in pieces] if has_dq else []),
            *([acc[b] for b in blocks] if has_acc else []),
        )
        for i, m in enumerate(pieces):
            dq[m] = result[i]
            if dq_done and m > 0:
                dq[m] = swap(dq[m], "head", m)
        for i, b in enumerate(blocks):
            acc[b] = result[len(pieces) + i]
            if acc_done and b > 0:
                acc[b] = trade(acc[b], b, levels)

    early = tuple(range(parts - 1))
    hops = use_order(levels)
    step((0,), (0,), False, False)
    step((1,), (0,), False, False)
    for b in hops[:-1]:
        step((0, 1), (b,), False, False)
    step(early[2:], (0, *hops[:-1]), False, False)
    step(early, (hops[-1],), True, False)
    for b in far_order(levels) + [0]:
        step((parts - 1,), (b,), b == 0, True)

    dkv = call(
        functools.partial(total_kernel, parts, levels),
        [
            vmem((2 * rows, HEAD_DIM), F32 if m == 0 else BF16) for m in range(parts)
        ],
        place,
        *acc,
    )
    dkv = [dkv[0]] + [swap(dkv[m], "head", m) for m in range(1, parts)]
    width = GROUP * HEAD_DIM

    def stage(count):
        return vmem((count, rows, width), F32)

    (grad_q,) = call(
        functools.partial(first_kernel, (0,)),
        [hbm(queries.shape, F32)],
        place,
        dq[0],
        out_space=pltpu.HBM,
        scratch=[stage(1), pltpu.SemaphoreType.DMA((1,))],
    )
    late = tuple(range(1, parts))
    (grad_q,) = call(
        functools.partial(more_kernel, late),
        [hbm(queries.shape, F32)],
        place,
        *[dq[m] for m in late],
        out_space=pltpu.HBM,
        filled=grad_q,
        scratch=[stage(len(late)), pltpu.SemaphoreType.DMA((len(late),))],
    )
    grad_k, grad_v = call(
        functools.partial(finish_kernel, parts),
        [hbm(key_rows.shape, F32), hbm(value_rows.shape, F32)],
        place,
        *dkv,
        out_space=pltpu.HBM,
        scratch=[
            vmem(key_rows.shape, F32),
            vmem(value_rows.shape, F32),
            pltpu.SemaphoreType.DMA((2,)),
        ],
    )
    return (grad_q, grad_k, grad_v)


def solution(mesh):
    rows = P(("ctx", "head"), None)
    return jax.shard_map(
        on_device,
        mesh=mesh,
        in_specs=(rows, rows, rows, rows, rows, P("head", "ctx")),
        out_specs=(rows, rows, rows),
        check_vma=False,
    )
```
